32 devices in a mesh: section: 4 (over z), rows: 8 (over y, x, core).
Axes of the slice: x: 2, y: 2, z: 4, core: 2. Of those that a mesh axis runs over, the one named last changes fastest.
Arguments:
- rows_data: float32 [16, 8192, 128], P('section', 'rows'), may hold values from -6 to 6
- row_keys: int32 [16, 8192], P('section', 'rows'), may hold values from 0 to 8191
- valid_counts: int32 [16, 8], P('section', 'rows'), may hold values from 256 to 1024
- predicates: int32 [4, 16, 256], P('section', None, 'rows'), may hold values from -2147483648 to 2147483647, as said below
- section_weight: float32 [4, 128, 128], P('section'), may hold values from -0.5 to 0.5
- section_bias: float32 [4, 128], P('section'), may hold values from -3 to 3
Outputs:
- key_means: float32 [8192, 128], P(('section', 'rows'))
- key_counts: float32 [8192], P(('section', 'rows'))
The draws below stay inside these ranges and needn't reach their ends.
Inputs may be any that keep to these rules, and one draw needn't show every extreme that they name: Bit j of predicates[s, m, w] is the flag of row 32 w + j of micro-batch m for section s; about three flags in four are 1. `row_keys`: keys are drawn from a skewed distribution: a few keys are very frequent and most are rare.
All inputs are finite; a program needn't handle non-finite values.
Results may differ from the reference program's by a relative error of at most 0.0001.
Values sent between devices are 32-bit elements; how exact they have to be, the bound alone decides.
No kernel may reach another device: no remote copies, remote signals or barrier semaphores. Data moves between devices by JAX's collectives and lax.ppermute only.
A program may use at most 64 MiB of HBM per device.

```python
import math
import jax
import jax.numpy as jnp
import numpy as np
from jax import lax

D = 128
KEYS = 8192
SECTIONS = 4
B_DEV = 1024
MICRO = 16
BROWS = 8192
N_ROWS = 8


def draw_predicates(key, part):
    shape = (SECTIONS, MICRO, BROWS // 32)
    first_key = jax.random.fold_in(key, 11)
    second_key = jax.random.fold_in(key, 23)
    lowest = -2147483647 - 1
    first = jax.random.randint(first_key, shape, lowest, 2147483647, dtype=jnp.int32)
    second = jax.random.randint(second_key, shape, lowest, 2147483647, dtype=jnp.int32)
    return first | second


def set_ends(result, key, least, high):
    index_at = [jax.random.randint(jax.random.fold_in(key, axis), (), 0, length) for axis, length in enumerate(result.shape)]
    widest = result.shape.index(max(result.shape))
    neighbour = index_at[:widest] + [(index_at[widest] + 1) % result.shape[widest]] + index_at[widest + 1:]
    return result.at[tuple(index_at)].set(least).at[tuple(neighbour)].set(high)


def block_scale(rng, extent, cuts, low, largest):
    def one(dim, blocks):
        steps = jax.random.uniform(jax.random.fold_in(jax.random.fold_in(rng, 6), dim), (blocks,), jnp.float32, low / len(cuts), largest / len(cuts))
        return jnp.repeat(jnp.exp(steps), extent[dim] // blocks).reshape((-1,) + (1,) * (len(extent) - dim - 1))

    factor_of = one(*cuts[0])
    for cut in cuts[1:]:
        factor_of = factor_of * one(*cut)
    return factor_of


def cumulative_ranks(count, slope):
    loads = [(1 << 20) // math.isqrt(rank ** slope) + 1 for rank in range(1, count + 1)]
    deviation = 1 + sum(loads) // (1 << 30)
    return np.cumsum(np.array([max(1, weight // deviation) for weight in loads]))


def ranked_ids(stream_key, extent, count, lean):
    table = cumulative_ranks(count, lean)
    ticket = jax.random.randint(jax.random.fold_in(stream_key, 1), extent, 0, int(table[count - 1]))
    rank = jnp.searchsorted(jnp.asarray(table, jnp.int32), ticket, side="right")
    return jax.random.permutation(jax.random.fold_in(stream_key, 2), count)[rank].astype(jnp.int32)


def noise(rng, extent, scale, limit, split=(), kind=jnp.bfloat16):
    entries = jax.random.normal(rng, extent, jnp.float32) * scale
    if len(split) > 0:
        entries = block_scale(rng, extent, split, -0.22, 0.18) * entries
    return jnp.clip(entries, min=-limit, max=limit).astype(kind)


def setup_inputs(seed: int = 0) -> dict:
    key_of = jax.random.split(jax.random.key(seed), 7)
    return {
        "rows_data": noise(key_of[0], (MICRO, BROWS, D), 1.0, 6.0, ((0, 4), (1, 8)), jnp.float32),
        "row_keys": set_ends(ranked_ids(key_of[1], (MICRO, BROWS), KEYS, 2), jax.random.fold_in(key_of[1], 3), 0, KEYS - 1).astype(jnp.int32),
        "valid_counts": set_ends(jax.random.randint(key_of[2], (MICRO, N_ROWS), B_DEV // 4, B_DEV + 1), jax.random.fold_in(key_of[2], 1), B_DEV // 4, B_DEV).astype(jnp.int32),
        "predicates": draw_predicates(jax.random.fold_in(key_of[6], 71), 0),
        "section_weight": noise(key_of[4], (SECTIONS, D, D), D ** -0.5, 0.5, ((0, 4),), jnp.float32),
        "section_bias": noise(key_of[5], (SECTIONS, D), 0.5, 3.0, ((0, 4),), jnp.float32),
    }


def advance(h, weight, bias):
    return h + jnp.tanh(jnp.dot(h, weight, precision=lax.Precision.HIGHEST, preferred_element_type=jnp.float32) + bias)


def unpack_flags(words):
    shifts = lax.broadcasted_iota(jnp.int32, (32,), 0)
    flags = jnp.right_shift(words[..., None], shifts) & 1
    return flags.reshape(words.shape[:-1] + (words.shape[-1] * 32,))


def reference(rows_data, row_keys, valid_counts, predicates, section_weight, section_bias):
    micro = rows_data.shape[0]
    brows = rows_data.shape[1]
    width = rows_data.shape[2]
    position = jnp.arange(brows, dtype=jnp.int32) % B_DEV
    limits = jnp.repeat(valid_counts, B_DEV, axis=1)
    alive = (position[None, :] < limits).reshape(-1)
    hidden = rows_data.reshape(micro * brows, width)
    keys = row_keys.reshape(-1)
    sums = jnp.zeros((KEYS, width), jnp.float32)
    counts = jnp.zeros((KEYS,), jnp.float32)
    for section in range(SECTIONS):
        alive = alive & (unpack_flags(predicates[section]).reshape(-1) == 1)
        hidden = advance(hidden, section_weight[section], section_bias[section])
        sums = sums + jax.ops.segment_sum(jnp.where(alive[:, None], hidden, 0.0), keys, num_segments=KEYS)
        counts = counts + jax.ops.segment_sum(alive.astype(jnp.float32), keys, num_segments=KEYS)
    key_means = sums / jnp.maximum(counts, 1.0)[:, None]
    return key_means, counts
```

```python
import functools
import jax
import jax.numpy as jnp
from jax import lax
from jax.experimental import pallas as pl
from jax.experimental.pallas import tpu as pltpu
from jax.sharding import PartitionSpec as P

KEYS = 8192
SECTIONS = 4
LANES = 128
BF16 = jnp.bfloat16
F32 = jnp.float32
VMEM = pl.BlockSpec(memory_space=pltpu.VMEM)
SMEM = pl.BlockSpec(memory_space=pltpu.SMEM)


def split(value):
    high = value.astype(BF16)
    return high, (value - high.astype(F32)).astype(BF16)


def iota(shape, axis):
    return lax.broadcasted_iota(jnp.int32, shape, axis)


class Plan:
    def __init__(self, mesh):
        self.sections = mesh.shape["section"]
        self.rows = mesh.shape["rows"]
        self.planes = self.rows.bit_length() - 2
        self.owned = KEYS // (self.sections * self.rows)
        self.color = self.owned // 2
        self.half = KEYS // 2
        self.send = self.half // 4
        bits = list(range(self.planes))
        turn = self.planes // 2
        self.orders = (bits, bits[turn:] + bits[:turn])

    def perm(self, row_xor, section_xor):
        return [
            (s * self.rows + r, (s ^ section_xor) * self.rows + (r ^ row_xor))
            for s in range(self.sections)
            for r in range(self.rows)
        ]


def slot_codes(plan, keys, z, p):
    log_color = plan.color.bit_length() - 1
    low = keys & (plan.color - 1)
    rest = keys >> log_color
    color = rest & 1
    core = (rest >> 1) & 1
    place = ((rest >> 2) & ((1 << plan.planes) - 1)) ^ p
    zrel = (rest >> (2 + plan.planes)) ^ z
    inner = []
    for order in plan.orders:
        index = 0
        for bit in order:
            index = index * 2 + (1 - ((place >> bit) & 1))
        inner.append(index)
    index = jnp.where(color == 0, inner[0], inner[1])
    count = 1 << (plan.planes - 1)
    kept = index >> (plan.planes - 1)
    index = index & (count - 1)
    slot = ((kept * 2 + color) * count + index) * plan.sections + zrel
    return slot * plan.color + low + core * plan.half


def advance_kernel(plan, x_ref, keys_ref, valid_ref, b0, b1, b2, b3, out_ref, count_ref, weight, bias, bytes_):
    batches, block, width = x_ref.shape
    z = lax.axis_index("section")
    row = lax.axis_index("rows")
    core = row & 1
    place = row >> 1
    bytes_[...] = jnp.zeros_like(bytes_)
    for k, buffer in enumerate((b0, b1, b2, b3)):
        level = z ^ k
        high, low = split(buffer[:width, :])
        weight[level, :width, :width] = high
        weight[level, width:, :width] = high
        weight[level, :width, width:] = low
        weight[level, width:, width:] = jnp.zeros_like(low)
        bytes_[level, :4, :] = buffer[width : width + 4, :]
        bias[level, :1, :] = buffer[width + 4 : width + 5, :]
    words = bytes_[...].reshape(SECTIONS * 8, LANES).astype(BF16)
    lane = iota((1, block), 1)
    table = jnp.zeros((2 * plan.half // LANES, LANES), F32)
    per_batch = block // LANES
    for m in range(batches):
        spread = (iota((LANES, block), 0) == (iota((LANES, block), 1) >> 5) + m * 32).astype(F32).astype(BF16)
        found = jnp.dot(words, spread, preferred_element_type=F32).astype(jnp.int32)
        which = (lane >> 3) & 3
        flags = []
        for s in range(SECTIONS):
            byte = found[8 * s : 8 * s + 1]
            for b in range(1, 4):
                byte = jnp.where(which == b, found[8 * s + b : 8 * s + b + 1], byte)
            flags.append((byte >> (lane & 7)) & 1)
        depth = flags[-1]
        for flag in flags[-2::-1]:
            depth = flag * (1 + depth)
        depth = jnp.where(lane < valid_ref[m, 0], depth, 0)
        code = slot_codes(plan, keys_ref[m : m + 1, :], z, place)
        code_f = code.astype(F32)
        for i in range(per_batch):
            at = batches * block + m * per_batch + i
            out_ref[at : at + 1, :] = code_f[:, i * LANES : (i + 1) * LANES]
        depth_f = depth.astype(F32)
        outer = (iota((2 * plan.half // LANES, block), 0) == (code >> 7)).astype(F32).astype(BF16)
        inner = jnp.where(iota((LANES, block), 0) == (code & (LANES - 1)), depth_f, 0.0).astype(BF16)
        table = table + lax.dot_general(outer, inner, (((1,), (1,)), ((), ())), preferred_element_type=F32)
        column = jnp.transpose(jnp.broadcast_to(depth_f, (8, block)))[:, :1]
        depth_b = jnp.broadcast_to(column, (block, width))
        hidden = x_ref[m]
        total = jnp.zeros((block, width), F32)
        for s in range(SECTIONS):
            both = jnp.concatenate(split(hidden), axis=1)
            product = jnp.dot(both, weight[s], preferred_element_type=F32)
            hidden = hidden + jnp.tanh(product[:, :width] + product[:, width:] + bias[s, :1, :])
            total = total + jnp.where(depth_b > s, hidden, 0.0)
        out_ref[m * block : (m + 1) * block, :] = total
    lines = plan.half // LANES
    first = core == 0
    at = batches * block + batches * per_batch
    count_ref[...] = jnp.where(first, table[:lines], table[lines:])
    out_ref[at : at + lines, :] = jnp.where(first, table[lines:], table[:lines])


def add_products(plan, source, first, slots, tile, piece, sums, core):
    values, codes = source
    rows = values.shape[0]
    base = (core * plan.half + first).astype(F32)
    for t in range(slots // tile):
        total = sums(t)
        for k in range(rows // piece):
            marks = []
            for i in range(piece // LANES):
                code = codes[k * piece // LANES + i : k * piece // LANES + i + 1, :] - base - float(t * tile)
                marks.append(jnp.where(code == iota((tile, LANES), 0).astype(F32), 1.0, 0.0).astype(BF16))
            mark = jnp.concatenate(marks, axis=1)
            total = total + jnp.dot(mark, values[k * piece : (k + 1) * piece, :], preferred_element_type=F32)
        yield t, total


def spread_rows(rows_ref, rows, scratch):
    high, low = split(rows_ref[:rows, :])
    width = high.shape[1]
    scratch[:, :width] = high
    scratch[:, width:] = low


def first_kernel(plan, rows, tile, piece, own_ref, out_ref, scratch):
    core = lax.axis_index("rows") & 1
    spread_rows(own_ref, rows, scratch)
    codes = own_ref.at[rows : rows + rows // LANES]
    width = out_ref.shape[1]
    for t, total in add_products(plan, (scratch, codes), 0, 2 * plan.send, tile, piece, lambda t: 0.0, core):
        out_ref[t * tile : (t + 1) * tile, :] = total[:, :width] + total[:, width:]


def second_kernel(plan, rows, tile, piece, other_ref, part_ref, count_ref, a_ref, b_ref, kept_ref, scratch):
    core = lax.axis_index("rows") & 1
    spread_rows(other_ref, rows, scratch)
    lines = rows // LANES
    codes = other_ref.at[rows : rows + lines]
    width = a_ref.shape[1]
    per = plan.send // tile
    for t, total in add_products(plan, (scratch, codes), 0, 2 * plan.send, tile, piece, lambda t: 0.0, core):
        target = (a_ref, b_ref)[t // per]
        at = (t % per) * tile
        target[at : at + tile, :] = total[:, :width] + total[:, width:] + part_ref[t * tile : (t + 1) * tile, :]
    counts = count_ref[...] + other_ref[rows + lines : rows + lines + plan.half // LANES, :]
    share = plan.send // LANES
    a_ref[plan.send :, :] = counts[:share]
    b_ref[plan.send :, :] = counts[share : 2 * share]
    kept_ref[...] = counts[2 * share :]


def third_kernel(plan, rows, tile, piece, own_ref, other_ref, count_ref, a_ref, b_ref, own_s, other_s):
    core = lax.axis_index("rows") & 1
    spread_rows(own_ref, rows, own_s)
    spread_rows(other_ref, rows, other_s)
    lines = rows // LANES
    width = a_ref.shape[1]
    per = plan.send // tile
    first = 2 * plan.send
    own = add_products(plan, (own_s, own_ref.at[rows : rows + lines]), first, first, tile, piece, lambda t: 0.0, core)
    held = {}

    def begin(t):
        held[t] = next(own)[1]
        return held[t]

    other = add_products(plan, (other_s, other_ref.at[rows : rows + lines]), first, first, tile, piece, begin, core)
    for t, total in other:
        target = (a_ref, b_ref)[t // per]
        at = (t % per) * tile
        target[at : at + tile, :] = total[:, :width] + total[:, width:]
    share = plan.send // LANES
    a_ref[plan.send :, :] = count_ref[:share]
    b_ref[plan.send :, :] = count_ref[share:]


def call(kernel, out_shape, operands, scratch=(), name=None, smem=()):
    return pl.pallas_call(
        kernel,
        out_shape=out_shape,
        in_specs=[SMEM if i in smem else VMEM for i in range(len(operands))],
        out_specs=jax.tree.map(lambda _: VMEM, out_shape),
        scratch_shapes=list(scratch),
        name=name,
    )(*operands)


def shape(*dims):
    return jax.ShapeDtypeStruct(dims, F32)


def shards(plan, rows_data, row_keys, valid_counts, predicates, section_weight, section_bias):
    batches, block, width = rows_data.shape
    axes = ("section", "rows")
    z = lax.axis_index("section")
    words = predicates.reshape(plan.sections, batches * predicates.shape[2])
    pieces = jnp.stack([(words >> (8 * b)) & 255 for b in range(4)], axis=1).astype(F32)
    buffers = []
    for k in range(plan.sections):
        part = lax.dynamic_index_in_dim(pieces, z ^ k, 0, keepdims=False)
        packed = jnp.concatenate([section_weight[0], part, section_bias, jnp.zeros((3, width), F32)], axis=0)
        if k:
            packed = lax.ppermute(packed, axes, plan.perm(0, k))
        buffers.append(packed)
    rows = batches * block
    lines = rows // LANES
    tables = plan.half // LANES
    own, count = call(
        functools.partial(advance_kernel, plan),
        (shape(rows + lines + tables, width), shape(tables, LANES)),
        (rows_data, row_keys, valid_counts, *buffers),
        scratch=[
            pltpu.VMEM((SECTIONS, 2 * width, 2 * width), BF16),
            pltpu.VMEM((SECTIONS, 8, width), F32),
            pltpu.VMEM((SECTIONS, 8, LANES), F32),
        ],
        name="advance",
        smem=(2,),
    )
    other = lax.ppermute(own, axes, plan.perm(1, 0))
    tile, piece = min(256, plan.send), min(1024, rows)
    wide = pltpu.VMEM((rows, 2 * width), BF16)
    part = call(
        functools.partial(first_kernel, plan, rows, tile, piece),
        shape(2 * plan.send, width),
        (own,),
        scratch=[wide],
        name="table_own",
    )
    share = plan.send // LANES
    message = shape(plan.send + share, width)
    send_a, send_b, kept_count = call(
        functools.partial(second_kernel, plan, rows, tile, piece),
        (message, message, shape(2 * share, LANES)),
        (other, part, count),
        scratch=[wide],
        name="table_send",
    )
    got = [lax.ppermute(m, axes, plan.perm(2 << order[0], 0)) for m, order in zip((send_a, send_b), plan.orders)]
    kept = call(
        functools.partial(third_kernel, plan, rows, tile, piece),
        (message, message),
        (own, other, kept_count),
        scratch=[wide, wide],
        name="table_keep",
    )
    states = []
    for color in range(2):
        total = kept[color] + got[color]
        states.append((total[: plan.send], total[plan.send :].reshape(-1)))
    for step in range(1, plan.planes):
        after = []
        for color in range(2):
            sums, counts = states[color]
            cut = sums.shape[0] // 2
            packed = jnp.concatenate([sums[:cut], counts[:cut].reshape(-1, LANES)], axis=0)
            moved = lax.ppermute(packed, axes, plan.perm(2 << plan.orders[color][step], 0))
            after.append((sums[cut:] + moved[:cut], counts[cut:] + moved[cut:].reshape(-1)))
        states = after
    sums = jnp.stack([s.reshape(plan.sections, plan.color, width) for s, _ in states], axis=1)
    counts = jnp.stack([c.reshape(plan.sections, plan.color) for _, c in states], axis=1)
    sums = sums.reshape(plan.sections, plan.owned, width)
    counts = counts.reshape(plan.sections, plan.owned)
    total, number = sums[0], counts[0]
    if plan.owned % LANES == 0:
        tail = counts.reshape(plan.sections, plan.owned // LANES, LANES)
    else:
        tail = jnp.pad(counts, ((0, 0), (0, LANES - plan.owned)))[:, None, :]
    for k in range(1, plan.sections):
        packed = jnp.concatenate([sums[k], tail[k]], axis=0)
        moved = lax.ppermute(packed, axes, plan.perm(0, k))
        total = total + moved[: plan.owned]
        number = number + moved[plan.owned :].reshape(-1)[: plan.owned]
    return total / jnp.maximum(number, 1.0)[:, None], number


def solution(mesh):
    return jax.shard_map(
        functools.partial(shards, Plan(mesh)),
        mesh=mesh,
        in_specs=(
            P("section", "rows", None),
            P("section", "rows"),
            P("section", "rows"),
            P("section", None, "rows"),
            P("section", None, None),
            P("section", None),
        ),
        out_specs=(P(("section", "rows"), None), P(("section", "rows"))),
        check_vma=False,
    )
```

```python
import functools
import jax
import jax.numpy as jnp
from jax import lax
from jax.experimental import pallas as pl
from jax.experimental.pallas import tpu as pltpu
from jax.sharding import PartitionSpec as P

KEYS = 8192
SECTIONS = 4
LANES = 128
BF16 = jnp.bfloat16
F32 = jnp.float32
VMEM = pl.BlockSpec(memory_space=pltpu.VMEM)
HBM = pl.BlockSpec(memory_space=pltpu.HBM)


def split(value):
    high = value.astype(BF16)
    return high, (value - high.astype(F32)).astype(BF16)


def iota(shape, axis):
    return lax.broadcasted_iota(jnp.int32, shape, axis)


class Plan:
    def __init__(self, mesh):
        self.sections = mesh.shape["section"]
        self.rows = mesh.shape["rows"]
        self.planes = self.rows.bit_length() - 2
        self.owned = KEYS // (self.sections * self.rows)
        self.color = self.owned // 2
        self.half = KEYS // 2
        self.send = self.half // 4
        bits = list(range(self.planes))
        turn = self.planes // 2
        self.orders = (bits, bits[turn:] + bits[:turn])

    def perm(self, row_xor, section_xor):
        return [
            (s * self.rows + r, (s ^ section_xor) * self.rows + (r ^ row_xor))
            for s in range(self.sections)
            for r in range(self.rows)
        ]


def slot_codes(plan, keys, z, p):
    log_color = plan.color.bit_length() - 1
    low = keys & (plan.color - 1)
    rest = keys >> log_color
    color = rest & 1
    core = (rest >> 1) & 1
    place = ((rest >> 2) & ((1 << plan.planes) - 1)) ^ p
    zrel = (rest >> (2 + plan.planes)) ^ z
    inner = []
    for order in plan.orders:
        index = 0
        for bit in order:
            index = index * 2 + (1 - ((place >> bit) & 1))
        inner.append(index)
    index = jnp.where(color == 0, inner[0], inner[1])
    count = 1 << (plan.planes - 1)
    kept = index >> (plan.planes - 1)
    index = index & (count - 1)
    slot = ((kept * 2 + color) * count + index) * plan.sections + zrel
    return slot * plan.color + low + core * plan.half


def fetch(pairs, sems):
    copies = [pltpu.make_async_copy(src, dst, sems.at[i]) for i, (src, dst) in enumerate(pairs)]
    for copy in copies:
        copy.start()
    return copies


def pack_kernel(plan, batches, predicates_hbm, weight_hbm, bias_hbm, *refs):
    buffers = refs[: plan.sections]
    predicates_ref, weight_ref, bias_ref, sems = refs[plan.sections :]
    copies = fetch(
        ((weight_hbm, weight_ref), (predicates_hbm, predicates_ref), (bias_hbm, bias_ref)),
        sems,
    )
    z = lax.axis_index("section")
    for copy in copies:
        copy.wait()
    width = weight_ref.shape[1]
    words_in_batch = predicates_ref.shape[2]
    for k, buffer in enumerate(buffers):
        buffer[:width, :] = weight_ref[0]
        buffer[width:, :] = jnp.zeros((buffer.shape[0] - width, width), F32)
        words = predicates_ref[0, pl.ds((z ^ k) * batches, batches), :]
        for b in range(4):
            at = width + b * batches
            buffer[at : at + batches, :words_in_batch] = ((words >> (8 * b)) & 255).astype(F32)
        at = width + 4 * batches
        buffer[at : at + 1, :] = bias_ref[...]


def advance_kernel(
    plan,
    x_hbm,
    keys_hbm,
    valid_hbm,
    b0,
    b1,
    b2,
    b3,
    out_ref,
    count_ref,
    x_ref,
    keys_ref,
    valid_ref,
    weight,
    bias,
    bytes_,
    sems,
):
    batches, block, width = x_hbm.shape
    keys_copy, valid_copy, *x_copies = fetch(
        ((keys_hbm, keys_ref), (valid_hbm, valid_ref), *((x_hbm.at[m], x_ref.at[m]) for m in range(batches))),
        sems,
    )
    z = lax.axis_index("section")
    row = lax.axis_index("rows")
    core = row & 1
    place = row >> 1
    for k, buffer in enumerate((b0, b1, b2, b3)):
        level = z ^ k
        high, low = split(buffer[:width, :])
        weight[level, :width, :width] = high
        weight[level, width:, :width] = high
        weight[level, :width, width:] = low
        weight[level, width:, width:] = jnp.zeros_like(low)
        bytes_[level] = buffer[width : width + 4 * batches, :]
        bias[level, :1, :] = buffer[width + 4 * batches : width + 4 * batches + 1, :]
    words = bytes_[...].reshape(SECTIONS * 4 * batches, LANES).astype(BF16)
    lane = iota((1, block), 1)
    spread = (iota((LANES, block), 0) == (iota((LANES, block), 1) >> 5)).astype(F32).astype(BF16)
    found = jnp.dot(words, spread, preferred_element_type=F32).astype(jnp.int32)
    which = (lane >> 3) & 3
    keys_copy.wait()
    valid_copy.wait()
    table = jnp.zeros((2 * plan.half // LANES, LANES), F32)
    per_batch = block // LANES
    for m in range(batches):
        flags = []
        for s in range(SECTIONS):
            at = s * 4 * batches + m
            byte = found[at : at + 1]
            for b in range(1, 4):
                byte = jnp.where(which == b, found[at + b * batches : at + b * batches + 1], byte)
            flags.append((byte >> (lane & 7)) & 1)
        depth = flags[-1]
        for flag in flags[-2::-1]:
            depth = flag * (1 + depth)
        depth = jnp.where(lane < valid_ref[:, m : m + 1], depth, 0)
        code = slot_codes(plan, keys_ref[m : m + 1, :], z, place)
        code_f = code.astype(F32)
        for i in range(per_batch):
            at = batches * block + m * per_batch + i
            out_ref[at : at + 1, :] = code_f[:, i * LANES : (i + 1) * LANES]
        depth_f = depth.astype(F32)
        outer = (iota((2 * plan.half // LANES, block), 0) == (code >> 7)).astype(F32).astype(BF16)
        inner = jnp.where(iota((LANES, block), 0) == (code & (LANES - 1)), depth_f, 0.0).astype(BF16)
        table = table + lax.dot_general(outer, inner, (((1,), (1,)), ((), ())), preferred_element_type=F32)
        column = jnp.transpose(jnp.broadcast_to(depth_f, (8, block)))[:, :1]
        depth_b = jnp.broadcast_to(column, (block, width))
        x_copies[m].wait()
        hidden = x_ref[m]
        total = jnp.zeros((block, width), F32)
        for s in range(SECTIONS):
            both = jnp.concatenate(split(hidden), axis=1)
            product = jnp.dot(both, weight[s], preferred_element_type=F32)
            hidden = hidden + jnp.tanh(product[:, :width] + product[:, width:] + bias[s, :1, :])
            total = total + jnp.where(depth_b > s, hidden, 0.0)
        out_ref[m * block : (m + 1) * block, :] = total
    lines = plan.half // LANES
    first = core == 0
    at = batches * block + batches * per_batch
    count_ref[...] = jnp.where(first, table[:lines], table[lines:])
    out_ref[at : at + lines, :] = jnp.where(first, table[lines:], table[:lines])


def add_products(plan, source, first, slots, tile, piece, sums, core):
    values, codes = source
    rows = values.shape[0]
    base = (core * plan.half + first).astype(F32)
    for t in range(slots // tile):
        total = sums(t)
        for k in range(rows // piece):
            marks = []
            for i in range(piece // LANES):
                code = codes[k * piece // LANES + i : k * piece // LANES + i + 1, :] - base - float(t * tile)
                marks.append(jnp.where(code == iota((tile, LANES), 0).astype(F32), 1.0, 0.0).astype(BF16))
            mark = jnp.concatenate(marks, axis=1)
            total = total + jnp.dot(mark, values[k * piece : (k + 1) * piece, :], preferred_element_type=F32)
        yield t, total


def spread_rows(rows_ref, rows, scratch):
    high, low = split(rows_ref[:rows, :])
    width = high.shape[1]
    scratch[:, :width] = high
    scratch[:, width:] = low


def first_kernel(plan, rows, tile, piece, own_ref, out_ref, scratch):
    core = lax.axis_index("rows") & 1
    spread_rows(own_ref, rows, scratch)
    codes = own_ref.at[rows : rows + rows // LANES]
    width = out_ref.shape[1]
    for t, total in add_products(plan, (scratch, codes), 0, 2 * plan.send, tile, piece, lambda t: 0.0, core):
        out_ref[t * tile : (t + 1) * tile, :] = total[:, :width] + total[:, width:]


def second_kernel(plan, rows, tile, piece, other_ref, part_ref, count_ref, a_ref, b_ref, kept_ref, scratch):
    core = lax.axis_index("rows") & 1
    spread_rows(other_ref, rows, scratch)
    lines = rows // LANES
    codes = other_ref.at[rows : rows + lines]
    width = a_ref.shape[1]
    per = plan.send // tile
    for t, total in add_products(plan, (scratch, codes), 0, 2 * plan.send, tile, piece, lambda t: 0.0, core):
        target = (a_ref, b_ref)[t // per]
        at = (t % per) * tile
        target[at : at + tile, :] = total[:, :width] + total[:, width:] + part_ref[t * tile : (t + 1) * tile, :]
    counts = count_ref[...] + other_ref[rows + lines : rows + lines + plan.half // LANES, :]
    share = plan.send // LANES
    a_ref[plan.send :, :] = counts[:share]
    b_ref[plan.send :, :] = counts[share : 2 * share]
    kept_ref[...] = counts[2 * share :]


def third_kernel(plan, rows, tile, piece, own_ref, other_ref, count_ref, a_ref, b_ref, own_s, other_s):
    core = lax.axis_index("rows") & 1
    spread_rows(own_ref, rows, own_s)
    spread_rows(other_ref, rows, other_s)
    lines = rows // LANES
    width = a_ref.shape[1]
    per = plan.send // tile
    first = 2 * plan.send
    own = add_products(plan, (own_s, own_ref.at[rows : rows + lines]), first, first, tile, piece, lambda t: 0.0, core)
    held = {}

    def begin(t):
        held[t] = next(own)[1]
        return held[t]

    other = add_products(plan, (other_s, other_ref.at[rows : rows + lines]), first, first, tile, piece, begin, core)
    for t, total in other:
        target = (a_ref, b_ref)[t // per]
        at = (t % per) * tile
        target[at : at + tile, :] = total[:, :width] + total[:, width:]
    share = plan.send // LANES
    a_ref[plan.send :, :] = count_ref[:share]
    b_ref[plan.send :, :] = count_ref[share:]


def call(kernel, out_shape, operands, scratch=(), name=None, hbm=(), limit=24):
    return pl.pallas_call(
        kernel,
        out_shape=out_shape,
        in_specs=[HBM if i in hbm else VMEM for i in range(len(operands))],
        out_specs=jax.tree.map(lambda _: VMEM, out_shape),
        scratch_shapes=list(scratch),
        name=name,
        compiler_params=pltpu.CompilerParams(vmem_limit_bytes=limit << 20),
    )(*(pltpu.with_memory_space_constraint(o, pltpu.HBM) if i in hbm else o for i, o in enumerate(operands)))


def shape(*dims):
    return jax.ShapeDtypeStruct(dims, F32)


def shards(plan, rows_data, row_keys, valid_counts, predicates, section_weight, section_bias):
    batches, block, width = rows_data.shape
    axes = ("section", "rows")
    packed = call(
        functools.partial(pack_kernel, plan, batches),
        (shape((width + 4 * batches + 8) // 8 * 8, width),) * plan.sections,
        (predicates, section_weight, section_bias),
        scratch=[
            pltpu.VMEM(predicates.shape, jnp.int32),
            pltpu.VMEM(section_weight.shape, F32),
            pltpu.VMEM(section_bias.shape, F32),
            pltpu.SemaphoreType.DMA((3,)),
        ],
        name="pack",
        hbm=(0, 1, 2),
        limit=4,
    )
    buffers = [packed[0]]
    for k in range(1, plan.sections):
        buffers.append(lax.ppermute(packed[k], axes, plan.perm(0, k)))
    rows = batches * block
    lines = rows // LANES
    tables = plan.half // LANES
    own, count = call(
        functools.partial(advance_kernel, plan),
        (shape(rows + lines + tables, width), shape(tables, LANES)),
        (rows_data, row_keys, valid_counts.reshape(1, batches), *buffers),
        scratch=[
            pltpu.VMEM((batches, block, width), F32),
            pltpu.VMEM((batches, block), jnp.int32),
            pltpu.VMEM((1, batches), jnp.int32),
            pltpu.VMEM((SECTIONS, 2 * width, 2 * width), BF16),
            pltpu.VMEM((SECTIONS, 8, width), F32),
            pltpu.VMEM((SECTIONS, 4 * batches, LANES), F32),
            pltpu.SemaphoreType.DMA((batches + 2,)),
        ],
        name="advance",
        hbm=(0, 1, 2),
    )
    other = lax.ppermute(own, axes, plan.perm(1, 0))
    tile, piece = min(256, plan.send), min(1024, rows)
    wide = pltpu.VMEM((rows, 2 * width), BF16)
    part = call(
        functools.partial(first_kernel, plan, rows, tile, piece),
        shape(2 * plan.send, width),
        (own,),
        scratch=[wide],
        name="table_own",
    )
    share = plan.send // LANES
    message = shape(plan.send + share, width)
    send_a, send_b, kept_count = call(
        functools.partial(second_kernel, plan, rows, tile, piece),
        (message, message, shape(2 * share, LANES)),
        (other, part, count),
        scratch=[wide],
        name="table_send",
    )
    got = [lax.ppermute(m, axes, plan.perm(2 << order[0], 0)) for m, order in zip((send_a, send_b), plan.orders)]
    kept = call(
        functools.partial(third_kernel, plan, rows, tile, piece),
        (message, message),
        (own, other, kept_count),
        scratch=[wide, wide],
        name="table_keep",
    )
    states = []
    for color in range(2):
        total = kept[color] + got[color]
        states.append((total[: plan.send], total[plan.send :].reshape(-1)))
    for step in range(1, plan.planes):
        after = []
        for color in range(2):
            sums, counts = states[color]
            cut = sums.shape[0] // 2
            packed = jnp.concatenate([sums[:cut], counts[:cut].reshape(-1, LANES)], axis=0)
            moved = lax.ppermute(packed, axes, plan.perm(2 << plan.orders[color][step], 0))
            after.append((sums[cut:] + moved[:cut], counts[cut:] + moved[cut:].reshape(-1)))
        states = after
    sums = jnp.stack([s.reshape(plan.sections, plan.color, width) for s, _ in states], axis=1)
    counts = jnp.stack([c.reshape(plan.sections, plan.color) for _, c in states], axis=1)
    sums = sums.reshape(plan.sections, plan.owned, width)
    counts = counts.reshape(plan.sections, plan.owned)
    total, number = sums[0], counts[0]
    if plan.owned % LANES == 0:
        tail = counts.reshape(plan.sections, plan.owned // LANES, LANES)
    else:
        tail = jnp.pad(counts, ((0, 0), (0, LANES - plan.owned)))[:, None, :]
    for k in range(1, plan.sections):
        packed = jnp.concatenate([sums[k], tail[k]], axis=0)
        moved = lax.ppermute(packed, axes, plan.perm(0, k))
        total = total + moved[: plan.owned]
        number = number + moved[plan.owned :].reshape(-1)[: plan.owned]
    return total / jnp.maximum(number, 1.0)[:, None], number


def solution(mesh):
    return jax.shard_map(
        functools.partial(shards, Plan(mesh)),
        mesh=mesh,
        in_specs=(
            P("section", "rows", None),
            P("section", "rows"),
            P("section", "rows"),
            P("section", None, "rows"),
            P("section", None, None),
            P("section", None),
        ),
        out_specs=(P(("section", "rows"), None), P(("section", "rows"))),
        check_vma=False,
    )
```

```python
import functools
import jax
import jax.numpy as jnp
from jax import lax
from jax.experimental import pallas as pl
from jax.experimental.pallas import tpu as pltpu
from jax.sharding import PartitionSpec as P

KEYS = 8192
STEP = 512
SECTIONS = 4
LANES = 128
BF16 = jnp.bfloat16
F32 = jnp.float32
VMEM = pl.BlockSpec(memory_space=pltpu.VMEM)
HBM = pl.BlockSpec(memory_space=pltpu.HBM)


def split(value):
    high = value.astype(BF16)
    return high, (value - high.astype(F32)).astype(BF16)


def iota(shape, axis):
    return lax.broadcasted_iota(jnp.int32, shape, axis)


class Plan:
    def __init__(self, mesh):
        self.sections = mesh.shape["section"]
        self.rows = mesh.shape["rows"]
        self.planes = self.rows.bit_length() - 2
        self.owned = KEYS // (self.sections * self.rows)
        self.color = self.owned // 2
        self.half = KEYS // 2
        self.inner = self.sections // 2
        self.chunk = self.half // 4
        bits = list(range(self.planes))
        turn = self.planes // 2
        self.orders = (bits, bits[turn:] + bits[:turn])

    def perm(self, row_xor, section_xor):
        return [
            (s * self.rows + r, (s ^ section_xor) * self.rows + (r ^ row_xor))
            for s in range(self.sections)
            for r in range(self.rows)
        ]


def slot_codes(plan, keys, z, p):
    log_color = plan.color.bit_length() - 1
    low = keys & (plan.color - 1)
    rest = keys >> log_color
    color = rest & 1
    core = (rest >> 1) & 1
    place = ((rest >> 2) & ((1 << plan.planes) - 1)) ^ p
    zrel = (rest >> (2 + plan.planes)) ^ z
    inner = []
    for order in plan.orders:
        index = 0
        for bit in order:
            index = index * 2 + (1 - ((place >> bit) & 1))
        inner.append(index)
    index = jnp.where(color == 0, inner[0], inner[1])
    count = 1 << (plan.planes - 1)
    kept = index >> (plan.planes - 1)
    near = 1 - zrel // plan.inner
    slot = ((near * 2 + kept) * 2 + color) * count + (index & (count - 1))
    return (slot * plan.inner + (zrel & (plan.inner - 1))) * plan.color + low + core * plan.half


def fetch(pairs, sems):
    copies = [pltpu.make_async_copy(src, dst, sems.at[i]) for i, (src, dst) in enumerate(pairs)]
    for copy in copies:
        copy.start()
    return copies


def pack_kernel(plan, batches, predicates_hbm, weight_hbm, bias_hbm, *refs):
    buffers = refs[: plan.sections]
    predicates_ref, weight_ref, bias_ref, sems = refs[plan.sections :]
    copies = fetch(
        ((weight_hbm, weight_ref), (predicates_hbm, predicates_ref), (bias_hbm, bias_ref)),
        sems,
    )
    z = lax.axis_index("section")
    for copy in copies:
        copy.wait()
    width = weight_ref.shape[1]
    words_in_batch = predicates_ref.shape[2]
    for k, buffer in enumerate(buffers):
        buffer[:width, :] = weight_ref[0]
        buffer[width:, :] = jnp.zeros((buffer.shape[0] - width, width), F32)
        words = predicates_ref[0, pl.ds((z ^ k) * batches, batches), :]
        for b in range(4):
            at = width + b * batches
            buffer[at : at + batches, :words_in_batch] = ((words >> (8 * b)) & 255).astype(F32)
        at = width + 4 * batches
        buffer[at : at + 1, :] = bias_ref[...]


def advance_kernel(
    plan,
    x_hbm,
    keys_hbm,
    valid_hbm,
    b0,
    b1,
    b2,
    b3,
    out_ref,
    count_ref,
    x_ref,
    keys_ref,
    valid_ref,
    weight,
    bias,
    bytes_,
    sparse,
    packed,
    lines_ref,
    table,
    sems,
):
    batches, block, width = x_hbm.shape
    keys_copy, valid_copy, *x_copies = fetch(
        ((keys_hbm, keys_ref), (valid_hbm, valid_ref), *((x_hbm.at[m], x_ref.at[m]) for m in range(batches))),
        sems,
    )
    z = lax.axis_index("section")
    row = lax.axis_index("rows")
    core = row & 1
    place = row >> 1
    for k, buffer in enumerate((b0, b1, b2, b3)):
        level = z ^ k
        high, low = split(buffer[:width, :])
        weight[level, :width, :width] = high
        weight[level, width:, :width] = high
        weight[level, :width, width:] = low
        weight[level, width:, width:] = jnp.zeros_like(low)
        bytes_[level] = buffer[width : width + 4 * batches, :]
        bias[level, :1, :] = buffer[width + 4 * batches : width + 4 * batches + 1, :]
    words = bytes_[...].reshape(SECTIONS * 4 * batches, LANES).astype(BF16)
    lane = iota((1, block), 1)
    spread = (iota((LANES, block), 0) == (iota((LANES, block), 1) >> 5)).astype(F32).astype(BF16)
    found = jnp.dot(words, spread, preferred_element_type=F32).astype(jnp.int32)
    which = (lane >> 3) & 3
    keys_copy.wait()
    valid_copy.wait()
    tile = sparse.shape[2]
    per_batch = block // tile
    for m in range(batches):
        flags = []
        for s in range(SECTIONS):
            at = s * 4 * batches + m
            byte = found[at : at + 1]
            for b in range(1, 4):
                byte = jnp.where(which == b, found[at + b * batches : at + b * batches + 1], byte)
            flags.append((byte >> (lane & 7)) & 1)
        depth = flags[-1]
        for flag in flags[-2::-1]:
            depth = flag * (1 + depth)
        depth = jnp.where(lane < valid_ref[:, m : m + 1], depth, 0).astype(F32)
        code = slot_codes(plan, keys_ref[m : m + 1, :], z, place).astype(F32)
        for q in range(per_batch):
            at = m * per_batch + q
            sparse[0, at : at + 1, :] = depth[:, q * tile : (q + 1) * tile]
            sparse[1, at : at + 1, :] = code[:, q * tile : (q + 1) * tile]

    depths = sparse[0]
    before = (iota((tile, tile), 0) < iota((tile, tile), 1)).astype(F32).astype(BF16)
    live = jnp.where(depths > 0.0, 1.0, 0.0)
    places = jnp.dot(live.astype(BF16), before, preferred_element_type=F32)
    places = jnp.where(depths > 0.0, places, -1.0)
    row8 = iota((8, tile), 0)
    lane8 = iota((8, LANES), 1)
    empty = jnp.where(iota((8, LANES), 0) == 0, -1.0, 0.0)
    for i in range(lines_ref.shape[0]):
        lines_ref[i] = empty
    offset = 0
    for m in range(batches):
        x_copies[m].wait()
        for q in range(per_batch):
            at = m * per_batch + q
            move = jnp.where(places[at : at + 1] == iota((tile, tile), 0).astype(F32), 1.0, 0.0).astype(BF16)
            both = jnp.concatenate(split(x_ref[m, q * tile : (q + 1) * tile, :]), axis=1)
            moved = jnp.dot(move, both, preferred_element_type=F32)
            packed[pl.ds(offset, tile), :] = moved[:, :width] + moved[:, width:]
            code = sparse[1, at : at + 1, :] + 1.0
            high = jnp.floor(code * (1.0 / LANES))
            info = jnp.where(row8 == 0, high, jnp.where(row8 == 1, code - high * LANES, 0.0))
            info = jnp.where(row8 == 2, sparse[0, at : at + 1, :], info).astype(BF16)
            info = lax.dot_general(info, move, (((1,), (1,)), ((), ())), preferred_element_type=F32)
            code = info[:1] * LANES + info[1:2] - 1.0
            info = jnp.where(row8 == 0, code, jnp.where(row8 == 1, info[2:3], 0.0))
            shift = offset & (LANES - 1)
            info = pltpu.roll(jnp.concatenate([info, empty], axis=1), shift, axis=1)
            line = offset // LANES
            lines_ref[line] = jnp.where(lane8 < shift, lines_ref[line], info[:, :LANES])
            for j in range(1, tile // LANES + 1):
                lines_ref[line + j] = info[:, j * LANES : (j + 1) * LANES]
            number = jnp.sum(live[at : at + 1]).astype(jnp.int32)
            offset = pl.multiple_of(offset + ((number + 7) // 8) * 8, 8)
    packed[pl.ds(offset, STEP), :] = jnp.zeros((STEP, width), F32)
    table[...] = jnp.zeros_like(table)

    def levels(step, _):
        at = pl.multiple_of(step * STEP, STEP)
        columns, codes, depths = [], [], []
        for j in range(STEP // LANES):
            line = lines_ref[step * (STEP // LANES) + j]
            columns.append(jnp.broadcast_to(jnp.transpose(line)[:, 1:2], (LANES, width)))
            codes.append(line[:1])
            depths.append(line[1:2])
        depth = jnp.concatenate(columns, axis=0)
        code = jnp.concatenate(codes, axis=1).astype(jnp.int32)
        outer = (iota((table.shape[0], STEP), 0) == (code >> 7)).astype(F32).astype(BF16)
        inner = iota((LANES, STEP), 0) == (code & (LANES - 1))
        inner = jnp.where(inner, jnp.concatenate(depths, axis=1), 0.0).astype(BF16)
        table[...] += lax.dot_general(outer, inner, (((1,), (1,)), ((), ())), preferred_element_type=F32)
        hidden = packed[pl.ds(at, STEP), :]
        total = jnp.zeros((STEP, width), F32)
        for s in range(SECTIONS):
            both = jnp.concatenate(split(hidden), axis=1)
            product = jnp.dot(both, weight[s], preferred_element_type=F32)
            hidden = hidden + jnp.tanh(product[:, :width] + product[:, width:] + bias[s, :1, :])
            total = total + jnp.where(depth > s, hidden, 0.0)
        out_ref[pl.ds(at, STEP), :] = total
        return 0

    lax.fori_loop(0, (offset + (STEP - 1)) // STEP, levels, 0)
    rows = batches * block
    for i in range(rows // LANES):
        out_ref[rows + i : rows + i + 1, :] = lines_ref[i, :1, :]
    lines = plan.half // LANES
    first = core == 0
    at = rows + rows // LANES
    count_ref[...] = jnp.where(first, table[:lines], table[lines:])
    out_ref[at : at + lines, :] = jnp.where(first, table[lines:], table[:lines])
    out_ref[at + lines :, :] = jnp.full((8, width), offset.astype(F32))


def add_products(plan, rows, source, first, slots, sums):
    core = lax.axis_index("rows") & 1
    base = (core * plan.half + first).astype(F32)
    used = jnp.max(source[source.shape[0] - 8 :, :]).astype(jnp.int32)
    tile = min(256, slots)
    sums[:slots, :] = jnp.zeros((slots, sums.shape[1]), F32)

    def body(step, _):
        at = pl.multiple_of(step * STEP, STEP)
        both = jnp.concatenate(split(source[pl.ds(at, STEP), :]), axis=1)
        codes = [source[pl.ds(rows + step * (STEP // LANES) + i, 1), :] - base for i in range(STEP // LANES)]
        for t in range(slots // tile):
            spots = (iota((tile, LANES), 0) + t * tile).astype(F32)
            marks = [jnp.where(code == spots, 1.0, 0.0).astype(BF16) for code in codes]
            mark = jnp.concatenate(marks, axis=1)
            sums[t * tile : (t + 1) * tile, :] += jnp.dot(mark, both, preferred_element_type=F32)
        return 0

    lax.fori_loop(0, (used + (STEP - 1)) // STEP, body, 0)


def own_kernel(plan, rows, own_ref, out_ref, sums):
    width = out_ref.shape[1]
    add_products(plan, rows, own_ref, 0, plan.half, sums)
    out_ref[...] = sums[:, :width] + sums[:, width:]


def other_kernel(plan, rows, first, other_ref, part_ref, count_ref, *refs):
    *outs, sums = refs
    width = part_ref.shape[1]
    size = plan.chunk // 2
    lines = size // LANES
    at = rows + rows // LANES
    for chunk, start in enumerate(first):
        add_products(plan, rows, other_ref, start, plan.chunk, sums)
        for color in range(2):
            out = outs[2 * chunk + color]
            low = color * size
            slot = start + low
            out[:size, :] = (
                sums[low : low + size, :width] + sums[low : low + size, width:] + part_ref[slot : slot + size, :]
            )
            line = slot // LANES
            out[size:, :] = count_ref[line : line + lines, :] + other_ref[at + line : at + line + lines, :]


def call(kernel, out_shape, operands, scratch=(), name=None, hbm=(), limit=24):
    return pl.pallas_call(
        kernel,
        out_shape=out_shape,
        in_specs=[HBM if i in hbm else VMEM for i in range(len(operands))],
        out_specs=jax.tree.map(lambda _: VMEM, out_shape),
        scratch_shapes=list(scratch),
        name=name,
        compiler_params=pltpu.CompilerParams(vmem_limit_bytes=limit << 20),
    )(*(pltpu.with_memory_space_constraint(o, pltpu.HBM) if i in hbm else o for i, o in enumerate(operands)))


def shape(*dims):
    return jax.ShapeDtypeStruct(dims, F32)


def lines_of(counts):
    return jnp.pad(counts, (0, -counts.shape[0] % LANES)).reshape(-1, LANES)


def shards(plan, rows_data, row_keys, valid_counts, predicates, section_weight, section_bias):
    batches, block, width = rows_data.shape
    axes = ("section", "rows")
    packed = call(
        functools.partial(pack_kernel, plan, batches),
        (shape((width + 4 * batches + 8) // 8 * 8, width),) * plan.sections,
        (predicates, section_weight, section_bias),
        scratch=[
            pltpu.VMEM(predicates.shape, jnp.int32),
            pltpu.VMEM(section_weight.shape, F32),
            pltpu.VMEM(section_bias.shape, F32),
            pltpu.SemaphoreType.DMA((3,)),
        ],
        name="pack",
        hbm=(0, 1, 2),
        limit=4,
    )
    buffers = [packed[0]]
    for k in range(1, plan.sections):
        buffers.append(lax.ppermute(packed[k], axes, plan.perm(0, k)))
    rows = batches * block
    lines = rows // LANES
    tables = plan.half // LANES
    tile = min(256, block)
    own, count = call(
        functools.partial(advance_kernel, plan),
        (shape(rows + lines + tables + 8, width), shape(tables, LANES)),
        (rows_data, row_keys, valid_counts.reshape(1, batches), *buffers),
        scratch=[
            pltpu.VMEM((batches, block, width), F32),
            pltpu.VMEM((batches, block), jnp.int32),
            pltpu.VMEM((1, batches), jnp.int32),
            pltpu.VMEM((SECTIONS, 2 * width, 2 * width), BF16),
            pltpu.VMEM((SECTIONS, 8, width), F32),
            pltpu.VMEM((SECTIONS, 4 * batches, LANES), F32),
            pltpu.VMEM((2, rows // tile, tile), F32),
            pltpu.VMEM((rows + STEP, width), F32),
            pltpu.VMEM((lines + STEP // LANES, 8, LANES), F32),
            pltpu.VMEM((2 * tables, LANES), F32),
            pltpu.SemaphoreType.DMA((batches + 2,)),
        ],
        name="advance",
        hbm=(0, 1, 2),
    )
    other = lax.ppermute(own, axes, plan.perm(1, 0))
    part = call(
        functools.partial(own_kernel, plan, rows),
        shape(plan.half, width),
        (own,),
        scratch=[pltpu.VMEM((plan.half, 2 * width), F32)],
        name="table_own",
    )
    size = plan.chunk // 2
    message = shape(size + size // LANES, width)

    def tables_of(name, *chunks, after=()):
        operand, _ = lax.optimization_barrier((part, tuple(after)))
        outs = call(
            functools.partial(other_kernel, plan, rows, [c * plan.chunk for c in chunks]),
            (message,) * (2 * len(chunks)),
            (other, operand, count),
            scratch=[pltpu.VMEM((plan.chunk, 2 * width), F32)],
            name=name,
        )
        return [outs[2 * i : 2 * i + 2] for i in range(len(chunks))]

    def halve(messages, step):
        return [
            lax.ppermute(m, axes, plan.perm(2 << order[step], 0)) for m, order in zip(messages, plan.orders)
        ]

    got = []
    for near in range(2):
        (sent,) = tables_of("table_far" if near == 0 else "table_near", 2 * near)
        got.append(halve(sent, 0))
    finals, sent = [], []
    for near in range(2):
        (kept,) = tables_of("keep_far" if near == 0 else "keep_near", 2 * near + 1, after=sent)
        states = []
        for color in range(2):
            total = kept[color] + got[near][color]
            states.append((total[:size], total[size:].reshape(-1)))
        sent = []
        for step in range(1, plan.planes):
            cut = states[0][0].shape[0] // 2
            packed = [jnp.concatenate([sums[:cut], lines_of(counts[:cut])], axis=0) for sums, counts in states]
            sent = sent or packed
            states = [
                (sums[cut:] + m[:cut], counts[cut:] + m[cut:].reshape(-1)[:cut])
                for (sums, counts), m in zip(states, halve(packed, step))
            ]
        sums = jnp.stack([s.reshape(plan.inner, plan.color, width) for s, _ in states], axis=1)
        counts = jnp.stack([c.reshape(plan.inner, plan.color) for _, c in states], axis=1)
        sums = sums.reshape(plan.inner, plan.owned, width)
        counts = counts.reshape(plan.inner, plan.owned)
        for i in range(plan.inner):
            k = (1 - near) * plan.inner + i
            packed = jnp.concatenate([sums[i], lines_of(counts[i])], axis=0)
            finals.append(lax.ppermute(packed, axes, plan.perm(0, k)) if k else packed)
    total = functools.reduce(jnp.add, finals)
    number = total[plan.owned :].reshape(-1)[: plan.owned]
    return total[: plan.owned] / jnp.maximum(number, 1.0)[:, None], number


def solution(mesh):
    return jax.shard_map(
        functools.partial(shards, Plan(mesh)),
        mesh=mesh,
        in_specs=(
            P("section", "rows", None),
            P("section", "rows"),
            P("section", "rows"),
            P("section", None, "rows"),
            P("section", None, None),
            P("section", None),
        ),
        out_specs=(P(("section", "rows"), None), P(("section", "rows"))),
        check_vma=False,
    )
```

```python
import functools
import jax
import jax.numpy as jnp
from jax import lax
from jax.experimental import pallas as pl
from jax.experimental.pallas import tpu as pltpu
from jax.sharding import PartitionSpec as P


KEYS = 8192
STEP = 512
SECTIONS = 4
LANES = 128
BF16 = jnp.bfloat16
F32 = jnp.float32
VMEM = pl.BlockSpec(memory_space=pltpu.VMEM)
HBM = pl.BlockSpec(memory_space=pltpu.HBM)


def split(value):
    high = value.astype(BF16)
    return high, (value - high.astype(F32)).astype(BF16)


def iota(shape, axis):
    return lax.broadcasted_iota(jnp.int32, shape, axis)


class Plan:
    def __init__(self, mesh):
        self.sections = mesh.shape["section"]
        self.rows = mesh.shape["rows"]
        self.planes = self.rows.bit_length() - 2
        self.owned = KEYS // (self.sections * self.rows)
        self.color = self.owned // 2
        self.half = KEYS // 2
        self.chunk = self.half // 4
        bits = list(range(self.planes))
        turn = self.planes // 2
        self.orders = (bits, bits[turn:] + bits[:turn])

    def perm(self, row_xor, section_xor):
        return [
            (s * self.rows + r, (s ^ section_xor) * self.rows + (r ^ row_xor))
            for s in range(self.sections)
            for r in range(self.rows)
        ]


def slot_codes(plan, keys, z, p):
    log_color = plan.color.bit_length() - 1
    low = keys & (plan.color - 1)
    rest = keys >> log_color
    color = rest & 1
    core = (rest >> 1) & 1
    place = ((rest >> 2) & ((1 << plan.planes) - 1)) ^ p
    zrel = (rest >> (2 + plan.planes)) ^ z
    inner = []
    for order in plan.orders:
        index = 0
        for bit in order:
            index = index * 2 + (1 - ((place >> bit) & 1))
        inner.append(index)
    index = jnp.where(color == 0, inner[0], inner[1])
    count = 1 << (plan.planes - 1)
    kept = index >> (plan.planes - 1)
    index = index & (count - 1)
    far = ((color * count + index) * 2 + (zrel & 1)) * plan.color + 2 * plan.chunk * kept
    near = ((kept * 2 + color) * count + index) * plan.color + jnp.where(zrel == 1, plan.chunk, 3 * plan.chunk)
    return jnp.where(zrel >= 2, far, near) + low + core * plan.half


def fetch(pairs, sems):
    copies = [pltpu.make_async_copy(src, dst, sems.at[i]) for i, (src, dst) in enumerate(pairs)]
    for copy in copies:
        copy.start()
    return copies


def pack_kernel(plan, batches, predicates_hbm, weight_hbm, bias_hbm, *refs):
    buffers = refs[: plan.sections]
    predicates_ref, weight_ref, bias_ref, sems = refs[plan.sections :]
    copies = fetch(
        ((weight_hbm, weight_ref), (predicates_hbm, predicates_ref), (bias_hbm, bias_ref)),
        sems,
    )
    z = lax.axis_index("section")
    for copy in copies:
        copy.wait()
    width = weight_ref.shape[1]
    words_in_batch = predicates_ref.shape[2]
    for k, buffer in enumerate(buffers):
        buffer[:width, :] = weight_ref[0]
        buffer[width:, :] = jnp.zeros((buffer.shape[0] - width, width), F32)
        words = predicates_ref[0, pl.ds((z ^ k) * batches, batches), :]
        words = jnp.concatenate([words[m : m + 1] for m in range(batches)], axis=1)
        for b in range(4):
            at = width + b
            buffer[at : at + 1, : batches * words_in_batch] = ((words >> (8 * b)) & 255).astype(F32)
        buffer[width + 4 : width + 5, :] = bias_ref[...]


def advance_kernel(
    plan,
    x_hbm,
    keys_hbm,
    valid_hbm,
    b0,
    b1,
    b2,
    b3,
    out_ref,
    count_ref,
    x_ref,
    keys_ref,
    valid_ref,
    weight,
    bias,
    bytes_,
    sparse,
    packed,
    lines_ref,
    table,
    sems,
):
    batches, block, width = x_hbm.shape
    keys_copy, valid_copy, *x_copies = fetch(
        ((keys_hbm, keys_ref), (valid_hbm, valid_ref), *((x_hbm.at[m], x_ref.at[m]) for m in range(batches))),
        sems,
    )
    z = lax.axis_index("section")
    row = lax.axis_index("rows")
    core = row & 1
    place = row >> 1
    for k, buffer in enumerate((b0, b1, b2, b3)):
        level = z ^ k
        high, low = split(buffer[:width, :])
        weight[level, :width, :width] = high
        weight[level, width:, :width] = high
        weight[level, :width, width:] = low
        weight[level, width:, width:] = jnp.zeros_like(low)
        bytes_[level] = buffer[width : width + 8, :]
        bias[level, :1, :] = buffer[width + 4 : width + 5, :]
    words = bytes_[...].reshape(SECTIONS * 8, LANES)
    turned = [pltpu.roll(words, (LANES - m * (block // 32)) % LANES, axis=1) for m in range(batches)]
    words = jnp.concatenate(turned, axis=0).astype(BF16)
    lane = iota((1, block), 1)
    spread = (iota((LANES, block), 0) == (iota((LANES, block), 1) >> 5)).astype(F32).astype(BF16)
    found = jnp.dot(words, spread, preferred_element_type=F32).astype(jnp.int32)
    which = (lane >> 3) & 3
    keys_copy.wait()
    valid_copy.wait()
    tile = sparse.shape[2]
    per_batch = block // tile
    for m in range(batches):
        flags = []
        for s in range(SECTIONS):
            at = (m * SECTIONS + s) * 8
            byte = found[at : at + 1]
            for b in range(1, 4):
                byte = jnp.where(which == b, found[at + b : at + b + 1], byte)
            flags.append((byte >> (lane & 7)) & 1)
        depth = flags[-1]
        for flag in flags[-2::-1]:
            depth = flag * (1 + depth)
        depth = jnp.where(lane < valid_ref[:, m : m + 1], depth, 0).astype(F32)
        code = slot_codes(plan, keys_ref[m : m + 1, :], z, place).astype(F32)
        for q in range(per_batch):
            at = m * per_batch + q
            sparse[0, at : at + 1, :] = depth[:, q * tile : (q + 1) * tile]
            sparse[1, at : at + 1, :] = code[:, q * tile : (q + 1) * tile]

    depths = sparse[0]
    before = (iota((tile, tile), 0) < iota((tile, tile), 1)).astype(F32).astype(BF16)
    live = jnp.where(depths > 0.0, 1.0, 0.0)
    places = jnp.dot(live.astype(BF16), before, preferred_element_type=F32)
    places = jnp.where(depths > 0.0, places, -1.0)
    row8 = iota((8, tile), 0)
    lane8 = iota((8, LANES), 1)
    empty = jnp.where(iota((8, LANES), 0) == 0, -1.0, 0.0)
    for i in range(lines_ref.shape[0]):
        lines_ref[i] = empty
    offset = 0
    for m in range(batches):
        x_copies[m].wait()
        for q in range(per_batch):
            at = m * per_batch + q
            move = jnp.where(places[at : at + 1] == iota((tile, tile), 0).astype(F32), 1.0, 0.0).astype(BF16)
            both = jnp.concatenate(split(x_ref[m, q * tile : (q + 1) * tile, :]), axis=1)
            moved = jnp.dot(move, both, preferred_element_type=F32)
            packed[pl.ds(offset, tile), :] = moved[:, :width] + moved[:, width:]
            code = sparse[1, at : at + 1, :] + 1.0
            high = jnp.floor(code * (1.0 / LANES))
            info = jnp.where(row8 == 0, high, jnp.where(row8 == 1, code - high * LANES, 0.0))
            info = jnp.where(row8 == 2, sparse[0, at : at + 1, :], info).astype(BF16)
            info = lax.dot_general(info, move, (((1,), (1,)), ((), ())), preferred_element_type=F32)
            code = info[:1] * LANES + info[1:2] - 1.0
            info = jnp.where(row8 == 0, code, jnp.where(row8 == 1, info[2:3], 0.0))
            shift = offset & (LANES - 1)
            info = pltpu.roll(jnp.concatenate([info, empty], axis=1), shift, axis=1)
            line = offset // LANES
            lines_ref[line] = jnp.where(lane8 < shift, lines_ref[line], info[:, :LANES])
            for j in range(1, tile // LANES + 1):
                lines_ref[line + j] = info[:, j * LANES : (j + 1) * LANES]
            number = jnp.sum(live[at : at + 1]).astype(jnp.int32)
            offset = pl.multiple_of(offset + ((number + 7) // 8) * 8, 8)
    packed[pl.ds(offset, STEP), :] = jnp.zeros((STEP, width), F32)
    table[...] = jnp.zeros_like(table)

    def levels(step, _):
        at = pl.multiple_of(step * STEP, STEP)
        columns, codes, depths = [], [], []
        for j in range(STEP // LANES):
            line = lines_ref[step * (STEP // LANES) + j]
            columns.append(jnp.broadcast_to(jnp.transpose(line)[:, 1:2], (LANES, width)))
            codes.append(line[:1])
            depths.append(line[1:2])
        depth = jnp.concatenate(columns, axis=0)
        code = jnp.concatenate(codes, axis=1).astype(jnp.int32)
        outer = (iota((table.shape[0], STEP), 0) == (code >> 7)).astype(F32).astype(BF16)
        inner = iota((LANES, STEP), 0) == (code & (LANES - 1))
        inner = jnp.where(inner, jnp.concatenate(depths, axis=1), 0.0).astype(BF16)
        table[...] += lax.dot_general(outer, inner, (((1,), (1,)), ((), ())), preferred_element_type=F32)
        hidden = packed[pl.ds(at, STEP), :]
        total = jnp.zeros((STEP, width), F32)
        for s in range(SECTIONS):
            both = jnp.concatenate(split(hidden), axis=1)
            product = jnp.dot(both, weight[s], preferred_element_type=F32)
            hidden = hidden + jnp.tanh(product[:, :width] + product[:, width:] + bias[s, :1, :])
            total = total + jnp.where(depth > s, hidden, 0.0)
        out_ref[pl.ds(at, STEP), :] = total
        return 0

    lax.fori_loop(0, (offset + (STEP - 1)) // STEP, levels, 0)
    rows = batches * block
    for i in range(rows // LANES):
        out_ref[rows + i : rows + i + 1, :] = lines_ref[i, :1, :]
    lines = plan.half // LANES
    first = core == 0
    at = rows + rows // LANES
    count_ref[...] = jnp.where(first, table[:lines], table[lines:])
    out_ref[at : at + lines, :] = jnp.where(first, table[lines:], table[:lines])
    out_ref[at + lines :, :] = jnp.full((8, width), offset.astype(F32))


def add_products(plan, rows, source, first, slots, sums):
    core = lax.axis_index("rows") & 1
    base = (core * plan.half + first).astype(F32)
    used = jnp.max(source[source.shape[0] - 8 :, :]).astype(jnp.int32)
    tile = min(256, slots)

    def body(step, _):
        at = pl.multiple_of(step * STEP, STEP)
        both = jnp.concatenate(split(source[pl.ds(at, STEP), :]), axis=1)
        codes = [source[pl.ds(rows + step * (STEP // LANES) + i, 1), :] - base for i in range(STEP // LANES)]
        for t in range(slots // tile):
            spots = (iota((tile, LANES), 0) + t * tile).astype(F32)
            marks = [jnp.where(code == spots, 1.0, 0.0).astype(BF16) for code in codes]
            mark = jnp.concatenate(marks, axis=1)
            sums[t * tile : (t + 1) * tile, :] += jnp.dot(mark, both, preferred_element_type=F32)
        return 0

    lax.fori_loop(0, (used + (STEP - 1)) // STEP, body, 0)


def own_kernel(plan, rows, own_ref, out_ref, sums):
    width = out_ref.shape[1]
    sums[...] = jnp.zeros_like(sums)
    add_products(plan, rows, own_ref, 0, sums.shape[0], sums)
    out_ref[...] = sums[:, :width] + sums[:, width:]


def table_kernel(plan, rows, start, early, other_ref, mine_ref, count_ref, *refs):
    *outs, sums = refs
    width = mine_ref.shape[1]
    size = plan.chunk // len(outs)
    lines = size // LANES
    at = rows + rows // LANES
    sums[...] = jnp.zeros_like(sums)
    if not early:
        add_products(plan, rows, mine_ref, start, plan.chunk, sums)
    add_products(plan, rows, other_ref, start, plan.chunk, sums)
    for i, out in enumerate(outs):
        low = i * size
        slot = start + low
        total = sums[low : low + size, :width] + sums[low : low + size, width:]
        out[:size, :] = total + mine_ref[slot : slot + size, :] if early else total
        line = slot // LANES
        out[size:, :] = count_ref[line : line + lines, :] + other_ref[at + line : at + line + lines, :]


def call(kernel, out_shape, operands, scratch=(), hbm=(), limit=24):
    return pl.pallas_call(
        kernel,
        out_shape=out_shape,
        in_specs=[HBM if i in hbm else VMEM for i in range(len(operands))],
        out_specs=jax.tree.map(lambda _: VMEM, out_shape),
        scratch_shapes=list(scratch),
        compiler_params=pltpu.CompilerParams(vmem_limit_bytes=limit << 20),
    )(*(pltpu.with_memory_space_constraint(o, pltpu.HBM) if i in hbm else o for i, o in enumerate(operands)))


def shape(*dims):
    return jax.ShapeDtypeStruct(dims, F32)


def lines_of(counts):
    return jnp.pad(counts, (0, -counts.shape[0] % LANES)).reshape(-1, LANES)


def shards(plan, rows_data, row_keys, valid_counts, predicates, section_weight, section_bias):
    batches, block, width = rows_data.shape
    axes = ("section", "rows")
    packed = call(
        functools.partial(pack_kernel, plan, batches),
        (shape(width + 8, width),) * plan.sections,
        (predicates, section_weight, section_bias),
        scratch=[
            pltpu.VMEM(predicates.shape, jnp.int32),
            pltpu.VMEM(section_weight.shape, F32),
            pltpu.VMEM(section_bias.shape, F32),
            pltpu.SemaphoreType.DMA((3,)),
        ],
        hbm=(0, 1, 2),
        limit=4,
    )
    buffers = [packed[0]]
    for k in range(1, plan.sections):
        buffers.append(lax.ppermute(packed[k], axes, plan.perm(0, k)))
    rows = batches * block
    lines = rows // LANES
    tables = plan.half // LANES
    tile = min(256, block)
    own, count = call(
        functools.partial(advance_kernel, plan),
        (shape(rows + lines + tables + 8, width), shape(tables, LANES)),
        (rows_data, row_keys, valid_counts.reshape(1, batches), *buffers),
        scratch=[
            pltpu.VMEM((batches, block, width), F32),
            pltpu.VMEM((batches, block), jnp.int32),
            pltpu.VMEM((1, batches), jnp.int32),
            pltpu.VMEM((SECTIONS, 2 * width, 2 * width), BF16),
            pltpu.VMEM((SECTIONS, 8, width), F32),
            pltpu.VMEM((SECTIONS, 8, LANES), F32),
            pltpu.VMEM((2, rows // tile, tile), F32),
            pltpu.VMEM((rows + STEP, width), F32),
            pltpu.VMEM((lines + STEP // LANES, 8, LANES), F32),
            pltpu.VMEM((2 * tables, LANES), F32),
            pltpu.SemaphoreType.DMA((batches + 2,)),
        ],
        hbm=(0, 1, 2),
    )
    other = lax.ppermute(own, axes, plan.perm(1, 0))
    part = call(
        functools.partial(own_kernel, plan, rows),
        shape(2 * plan.chunk, width),
        (own,),
        scratch=[pltpu.VMEM((2 * plan.chunk, 2 * width), F32)],
    )

    def table(chunk, messages, after=()):
        size = plan.chunk // messages
        early = chunk < 2
        operand, _ = lax.optimization_barrier((count, tuple(after)))
        return call(
            functools.partial(table_kernel, plan, rows, chunk * plan.chunk, early),
            (shape(size + size // LANES, width),) * messages,
            (other, part if early else own, operand),
            scratch=[pltpu.VMEM((plan.chunk, 2 * width), F32)],
        )

    def open_message(message, size):
        return message[:size], message[size:].reshape(-1)[:size]

    def close_message(sums, counts):
        return jnp.concatenate([sums, lines_of(counts)], axis=0)

    def send(message, row_xor, section_xor):
        return lax.ppermute(message, axes, plan.perm(row_xor, section_xor))

    def swap(messages, step):
        return [send(m, 2 << order[step], 0) for m, order in zip(messages, plan.orders)]

    def halve(states, step):
        cut = states[0][0].shape[0] // 2
        packed = [close_message(sums[:cut], counts[:cut]) for sums, counts in states]
        moved = [open_message(m, cut) for m in swap(packed, step)]
        return packed, [(s[cut:] + a, c[cut:] + b) for (s, c), (a, b) in zip(states, moved)]

    size = plan.chunk // 2
    got = swap(table(0, 2), 0)
    sent = table(1, 1)
    near = send(sent[0], 0, 1)
    far = [open_message(k + g, size) for k, g in zip(table(2, 2, after=sent), got)]
    gate = ()
    for step in range(1, plan.planes):
        packed, far = halve(far, step)
        gate = gate or packed
    sums = jnp.stack([s.reshape(2, plan.color, width) for s, _ in far], axis=1).reshape(2, plan.owned, width)
    counts = jnp.stack([c.reshape(2, plan.color) for _, c in far], axis=1).reshape(2, plan.owned)
    finals = [send(close_message(sums[i], counts[i]), 0, 2 + i) for i in range(2)]
    (kept,) = table(3, 1, after=gate)
    near = kept + near
    sums, counts = open_message(near, plan.chunk)
    sums = sums.reshape(2, 2, size // 2, width)
    counts = counts.reshape(2, 2, size // 2)
    states = [(sums[:, c].reshape(size, width), counts[:, c].reshape(size)) for c in range(2)]
    for step in range(plan.planes):
        _, states = halve(states, step)
    finals.append(close_message(jnp.concatenate([s for s, _ in states]), jnp.concatenate([c for _, c in states])))
    total = functools.reduce(jnp.add, finals)
    number = total[plan.owned :].reshape(-1)[: plan.owned]
    return total[: plan.owned] / jnp.maximum(number, 1.0)[:, None], number


def solution(mesh):
    plan = Plan(mesh)

    def body(*args):
        return shards(plan, *args)

    return jax.shard_map(
        body,
        mesh=mesh,
        in_specs=(
            P("section", "rows", None),
            P("section", "rows"),
            P("section", "rows"),
            P("section", None, "rows"),
            P("section", None, None),
            P("section", None),
        ),
        out_specs=(P(("section", "rows"), None), P(("section", "rows"))),
        check_vma=False,
    )
```

```python
import functools
import jax
import jax.numpy as jnp
from jax import lax
from jax.experimental import pallas as pl
from jax.experimental.pallas import tpu as pltpu
from jax.sharding import PartitionSpec as P


KEYS = 8192
STEP = 512
LEVEL = 1024
SECTIONS = 4
LANES = 128
BF16 = jnp.bfloat16
F32 = jnp.float32
VMEM = pl.BlockSpec(memory_space=pltpu.VMEM)
HBM = pl.BlockSpec(memory_space=pltpu.HBM)


def split(value):
    high = value.astype(BF16)
    return high, (value - high.astype(F32)).astype(BF16)


def iota(shape, axis):
    return lax.broadcasted_iota(jnp.int32, shape, axis)


class Plan:
    def __init__(self, mesh):
        self.sections = mesh.shape["section"]
        self.rows = mesh.shape["rows"]
        self.planes = self.rows.bit_length() - 2
        self.owned = KEYS // (self.sections * self.rows)
        self.color = self.owned // 2
        self.half = KEYS // 2
        self.chunk = self.half // 4
        bits = list(range(self.planes))
        turn = self.planes // 2
        self.orders = (bits, bits[turn:] + bits[:turn])

    def perm(self, row_xor, section_xor):
        return [
            (s * self.rows + r, (s ^ section_xor) * self.rows + (r ^ row_xor))
            for s in range(self.sections)
            for r in range(self.rows)
        ]


def slot_codes(plan, keys, z, p):
    log_color = plan.color.bit_length() - 1
    low = keys & (plan.color - 1)
    rest = keys >> log_color
    color = rest & 1
    core = (rest >> 1) & 1
    place = ((rest >> 2) & ((1 << plan.planes) - 1)) ^ p
    zrel = (rest >> (2 + plan.planes)) ^ z
    inner = []
    for order in plan.orders:
        index = 0
        for bit in order:
            index = index * 2 + (1 - ((place >> bit) & 1))
        inner.append(index)
    index = jnp.where(color == 0, inner[0], inner[1])
    count = 1 << (plan.planes - 1)
    kept = index >> (plan.planes - 1)
    index = index & (count - 1)
    far = ((color * count + index) * 2 + (zrel & 1)) * plan.color + 2 * plan.chunk * kept
    near = ((kept * 2 + color) * count + index) * plan.color + jnp.where(zrel == 1, plan.chunk, 3 * plan.chunk)
    return jnp.where(zrel >= 2, far, near) + low + core * plan.half


def fetch(pairs, sems):
    copies = [pltpu.make_async_copy(src, dst, sems.at[i]) for i, (src, dst) in enumerate(pairs)]
    for copy in copies:
        copy.start()
    return copies


def pack_kernel(plan, batches, predicates_hbm, weight_hbm, bias_hbm, *refs):
    buffers = refs[: plan.sections]
    predicates_ref, weight_ref, bias_ref, sems = refs[plan.sections :]
    copies = fetch(
        ((weight_hbm, weight_ref), (predicates_hbm, predicates_ref), (bias_hbm, bias_ref)),
        sems,
    )
    z = lax.axis_index("section")
    for copy in copies:
        copy.wait()
    width = weight_ref.shape[1]
    words_in_batch = predicates_ref.shape[2]
    for k, buffer in enumerate(buffers):
        buffer[:width, :] = weight_ref[0]
        buffer[width:, :] = jnp.zeros((buffer.shape[0] - width, width), F32)
        words = predicates_ref[0, pl.ds((z ^ k) * batches, batches), :]
        words = jnp.concatenate([words[m : m + 1] for m in range(batches)], axis=1)
        for b in range(4):
            at = width + b
            buffer[at : at + 1, : batches * words_in_batch] = ((words >> (8 * b)) & 255).astype(F32)
        buffer[width + 4 : width + 5, :] = bias_ref[...]


def advance_kernel(
    plan,
    x_hbm,
    keys_hbm,
    valid_hbm,
    b0,
    b1,
    b2,
    b3,
    out_ref,
    own_packed,
    own_lines,
    weight,
    bias,
    x_ref,
    keys_ref,
    valid_ref,
    bytes_,
    sparse,
    out_packed,
    out_lines,
    sems,
):
    batches, block, width = x_hbm.shape
    keys_copy, valid_copy, *x_copies = fetch(
        ((keys_hbm, keys_ref), (valid_hbm, valid_ref), *((x_hbm.at[m], x_ref.at[m]) for m in range(batches))),
        sems,
    )
    z = lax.axis_index("section")
    row = lax.axis_index("rows")
    core = row & 1
    place = row >> 1
    for k, buffer in enumerate((b0, b1, b2, b3)):
        level = z ^ k
        high, low = split(buffer[:width, :])
        weight[level, :width, :width] = high
        weight[level, width:, :width] = high
        weight[level, :width, width:] = low
        weight[level, width:, width:] = jnp.zeros_like(low)
        bytes_[level] = buffer[width : width + 8, :]
        bias[level, :1, :] = buffer[width + 4 : width + 5, :]
    words = bytes_[...].reshape(SECTIONS * 8, LANES)
    turned = [pltpu.roll(words, (LANES - m * (block // 32)) % LANES, axis=1) for m in range(batches)]
    words = jnp.concatenate(turned, axis=0).astype(BF16)
    lane = iota((1, block), 1)
    spread = (iota((LANES, block), 0) == (iota((LANES, block), 1) >> 5)).astype(F32).astype(BF16)
    found = jnp.dot(words, spread, preferred_element_type=F32).astype(jnp.int32)
    which = (lane >> 3) & 3
    keys_copy.wait()
    valid_copy.wait()
    tile = sparse.shape[2]
    per_batch = block // tile
    for m in range(batches):
        flags = []
        for s in range(SECTIONS):
            at = (m * SECTIONS + s) * 8
            byte = found[at : at + 1]
            for b in range(1, 4):
                byte = jnp.where(which == b, found[at + b : at + b + 1], byte)
            flags.append((byte >> (lane & 7)) & 1)
        depth = flags[-1]
        for flag in flags[-2::-1]:
            depth = flag * (1 + depth)
        depth = jnp.where(lane < valid_ref[:, m : m + 1], depth, 0).astype(F32)
        code = slot_codes(plan, keys_ref[m : m + 1, :], z, place).astype(F32)
        for q in range(per_batch):
            at = m * per_batch + q
            sparse[0, at : at + 1, :] = depth[:, q * tile : (q + 1) * tile]
            sparse[1, at : at + 1, :] = code[:, q * tile : (q + 1) * tile]

    depths = sparse[0]
    here = jnp.where(sparse[1] >= plan.half, 1.0, 0.0) == core.astype(F32)
    before = (iota((tile, tile), 0) < iota((tile, tile), 1)).astype(F32).astype(BF16)
    lists = []
    for same in (here, jnp.logical_not(here)):
        live = jnp.where(jnp.logical_and(depths > 0.0, same), 1.0, 0.0)
        places = jnp.dot(live.astype(BF16), before, preferred_element_type=F32)
        lists.append((live, jnp.where(live > 0.0, places, -1.0)))
    row8 = iota((8, tile), 0)
    lane8 = iota((8, LANES), 1)
    empty = jnp.where(iota((8, LANES), 0) == 0, -1.0, 0.0)
    packed, lines_refs = (own_packed, out_packed), (own_lines, out_lines)
    for lines_ref in lines_refs:
        for i in range(lines_ref.shape[0]):
            lines_ref[i] = empty
    offsets = [0, 0]
    for m in range(batches):
        x_copies[m].wait()
        for q in range(per_batch):
            at = m * per_batch + q
            spots = iota((tile, tile), 0).astype(F32)
            moves = [jnp.where(places[at : at + 1] == spots, 1.0, 0.0).astype(BF16) for _, places in lists]
            move = jnp.concatenate(moves, axis=0)
            both = jnp.concatenate(split(x_ref[m, q * tile : (q + 1) * tile, :]), axis=1)
            moved = jnp.dot(move, both, preferred_element_type=F32)
            moved = moved[:, :width] + moved[:, width:]
            code = sparse[1, at : at + 1, :] + 1.0
            high = jnp.floor(code * (1.0 / LANES))
            info = jnp.where(row8 == 0, high, jnp.where(row8 == 1, code - high * LANES, 0.0))
            info = jnp.where(row8 == 2, sparse[0, at : at + 1, :], info).astype(BF16)
            infos = lax.dot_general(info, move, (((1,), (1,)), ((), ())), preferred_element_type=F32)
            for l, (live, _) in enumerate(lists):
                offset = offsets[l]
                packed[l][pl.ds(offset, tile), :] = moved[l * tile : (l + 1) * tile]
                info = infos[:, l * tile : (l + 1) * tile]
                code = info[:1] * LANES + info[1:2] - 1.0
                info = jnp.where(row8 == 0, code, jnp.where(row8 == 1, info[2:3], 0.0))
                shift = offset & (LANES - 1)
                info = pltpu.roll(jnp.concatenate([info, empty], axis=1), shift, axis=1)
                line = offset // LANES
                lines_ref = lines_refs[l]
                lines_ref[line] = jnp.where(lane8 < shift, lines_ref[line], info[:, :LANES])
                for j in range(1, tile // LANES + 1):
                    lines_ref[line + j] = info[:, j * LANES : (j + 1) * LANES]
                number = jnp.sum(live[at : at + 1]).astype(jnp.int32)
                offsets[l] = pl.multiple_of(offset + ((number + 7) // 8) * 8, 8)
    for l in range(2):
        packed[l][pl.ds(offsets[l], LEVEL), :] = jnp.zeros((LEVEL, width), F32)
    used = jnp.full((8, width), offsets[0].astype(F32))
    own_lines[own_lines.shape[0] - 1] = used
    used = offsets[1]
    out_ref[out_ref.shape[0] - 8 :, :] = jnp.full((8, width), used.astype(F32))
    rows = batches * block
    lines = rows // LANES
    counts = out_ref.at[rows + lines : rows + lines + plan.half // LANES]
    run_levels(plan, rows, 1 - core, used, out_packed, out_lines, weight, bias, out_ref, counts)


def run_levels(plan, rows, core, used, packed, lines_ref, weight, bias, target, counts):
    width = target.shape[1]
    counts[...] = jnp.zeros(counts.shape, F32)

    def body(step, _):
        at = pl.multiple_of(step * LEVEL, LEVEL)
        columns, codes, depths = [], [], []
        for j in range(LEVEL // LANES):
            line = lines_ref[step * (LEVEL // LANES) + j]
            columns.append(jnp.broadcast_to(jnp.transpose(line)[:, 1:2], (LANES, width)))
            codes.append(line[:1])
            depths.append(line[1:2])
        depth = jnp.concatenate(columns, axis=0)
        code = jnp.concatenate(codes, axis=1).astype(jnp.int32) - core * plan.half
        outer = (iota((counts.shape[0], LEVEL), 0) == (code >> 7)).astype(F32).astype(BF16)
        inner = iota((LANES, LEVEL), 0) == (code & (LANES - 1))
        inner = jnp.where(inner, jnp.concatenate(depths, axis=1), 0.0).astype(BF16)
        counts[...] += lax.dot_general(outer, inner, (((1,), (1,)), ((), ())), preferred_element_type=F32)
        hidden = packed[pl.ds(at, LEVEL), :]
        total = jnp.zeros((LEVEL, width), F32)
        for s in range(SECTIONS):
            both = jnp.concatenate(split(hidden), axis=1)
            product = jnp.dot(both, weight[s], preferred_element_type=F32)
            hidden = hidden + jnp.tanh(product[:, :width] + product[:, width:] + bias[s, :1, :])
            total = total + jnp.where(depth > s, hidden, 0.0)
        target[pl.ds(at, LEVEL), :] = total
        return 0

    lax.fori_loop(0, (used + (LEVEL - 1)) // LEVEL, body, 0)
    for i in range(rows // LANES):
        target[rows + i : rows + i + 1, :] = lines_ref[i, :1, :]


def own_levels_kernel(plan, rows, packed, lines_ref, weight, bias, own_ref, counts):
    core = lax.axis_index("rows") & 1
    used = lines_ref[lines_ref.shape[0] - 1]
    own_ref[own_ref.shape[0] - 8 :, :] = used
    used = jnp.max(used).astype(jnp.int32)
    run_levels(plan, rows, core, used, packed, lines_ref, weight, bias, own_ref, counts)


def add_products(plan, rows, source, first, slots, sums):
    core = lax.axis_index("rows") & 1
    base = (core * plan.half + first).astype(F32)
    used = jnp.max(source[source.shape[0] - 8 :, :]).astype(jnp.int32)
    tile = min(256, slots)

    def body(step, _):
        at = pl.multiple_of(step * STEP, STEP)
        both = jnp.concatenate(split(source[pl.ds(at, STEP), :]), axis=1)
        codes = [source[pl.ds(rows + step * (STEP // LANES) + i, 1), :] - base for i in range(STEP // LANES)]
        for t in range(slots // tile):
            spots = (iota((tile, LANES), 0) + t * tile).astype(F32)
            marks = [jnp.where(code == spots, 1.0, 0.0).astype(BF16) for code in codes]
            mark = jnp.concatenate(marks, axis=1)
            sums[t * tile : (t + 1) * tile, :] += jnp.dot(mark, both, preferred_element_type=F32)
        return 0

    lax.fori_loop(0, (used + (STEP - 1)) // STEP, body, 0)


def own_kernel(plan, rows, own_ref, out_ref, sums):
    width = out_ref.shape[1]
    sums[...] = jnp.zeros_like(sums)
    add_products(plan, rows, own_ref, 0, sums.shape[0], sums)
    out_ref[...] = sums[:, :width] + sums[:, width:]


def table_kernel(plan, rows, start, early, other_ref, mine_ref, count_ref, *refs):
    *outs, sums = refs
    width = mine_ref.shape[1]
    size = plan.chunk // len(outs)
    lines = size // LANES
    at = rows + rows // LANES
    sums[...] = jnp.zeros_like(sums)
    if not early:
        add_products(plan, rows, mine_ref, start, plan.chunk, sums)
    add_products(plan, rows, other_ref, start, plan.chunk, sums)
    for i, out in enumerate(outs):
        low = i * size
        slot = start + low
        total = sums[low : low + size, :width] + sums[low : low + size, width:]
        out[:size, :] = total + mine_ref[slot : slot + size, :] if early else total
        line = slot // LANES
        out[size:, :] = count_ref[line : line + lines, :] + other_ref[at + line : at + line + lines, :]


def call(kernel, out_shape, operands, scratch=(), hbm=(), limit=24):
    return pl.pallas_call(
        kernel,
        out_shape=out_shape,
        in_specs=[HBM if i in hbm else VMEM for i in range(len(operands))],
        out_specs=jax.tree.map(lambda _: VMEM, out_shape),
        scratch_shapes=list(scratch),
        compiler_params=pltpu.CompilerParams(vmem_limit_bytes=limit << 20),
    )(*(pltpu.with_memory_space_constraint(o, pltpu.HBM) if i in hbm else o for i, o in enumerate(operands)))


def shape(*dims):
    return jax.ShapeDtypeStruct(dims, F32)


def lines_of(counts):
    return jnp.pad(counts, (0, -counts.shape[0] % LANES)).reshape(-1, LANES)


def shards(plan, rows_data, row_keys, valid_counts, predicates, section_weight, section_bias):
    batches, block, width = rows_data.shape
    axes = ("section", "rows")
    packed = call(
        functools.partial(pack_kernel, plan, batches),
        (shape(width + 8, width),) * plan.sections,
        (predicates, section_weight, section_bias),
        scratch=[
            pltpu.VMEM(predicates.shape, jnp.int32),
            pltpu.VMEM(section_weight.shape, F32),
            pltpu.VMEM(section_bias.shape, F32),
            pltpu.SemaphoreType.DMA((3,)),
        ],
        hbm=(0, 1, 2),
        limit=4,
    )
    buffers = [packed[0]]
    for k in range(1, plan.sections):
        buffers.append(lax.ppermute(packed[k], axes, plan.perm(0, k)))
    rows = batches * block
    lines = rows // LANES
    tables = plan.half // LANES
    tile = min(256, block)
    listed = (shape(rows + LEVEL, width), shape(lines + LEVEL // LANES + 1, 8, LANES))
    given, *mine = call(
        functools.partial(advance_kernel, plan),
        (
            shape(rows + lines + tables + 8, width),
            *listed,
            jax.ShapeDtypeStruct((SECTIONS, 2 * width, 2 * width), BF16),
            shape(SECTIONS, 8, width),
        ),
        (rows_data, row_keys, valid_counts.reshape(1, batches), *buffers),
        scratch=[
            pltpu.VMEM((batches, block, width), F32),
            pltpu.VMEM((batches, block), jnp.int32),
            pltpu.VMEM((1, batches), jnp.int32),
            pltpu.VMEM((SECTIONS, 8, LANES), F32),
            pltpu.VMEM((2, rows // tile, tile), F32),
            *(pltpu.VMEM(one.shape, F32) for one in listed),
            pltpu.SemaphoreType.DMA((batches + 2,)),
        ],
        hbm=(0, 1, 2),
    )
    other = lax.ppermute(given, axes, plan.perm(1, 0))
    own, count = call(
        functools.partial(own_levels_kernel, plan, rows), (shape(rows + lines + 8, width), shape(tables, LANES)), mine
    )
    part = call(
        functools.partial(own_kernel, plan, rows),
        shape(2 * plan.chunk, width),
        (own,),
        scratch=[pltpu.VMEM((2 * plan.chunk, 2 * width), F32)],
    )

    def table(chunk, messages, after=()):
        size = plan.chunk // messages
        early = chunk < 2
        operand, _ = lax.optimization_barrier((count, tuple(after)))
        return call(
            functools.partial(table_kernel, plan, rows, chunk * plan.chunk, early),
            (shape(size + size // LANES, width),) * messages,
            (other, part if early else own, operand),
            scratch=[pltpu.VMEM((plan.chunk, 2 * width), F32)],
        )

    def open_message(message, size):
        return message[:size], message[size:].reshape(-1)[:size]

    def close_message(sums, counts):
        return jnp.concatenate([sums, lines_of(counts)], axis=0)

    def send(message, row_xor, section_xor):
        return lax.ppermute(message, axes, plan.perm(row_xor, section_xor))

    def swap(messages, step):
        return [send(m, 2 << order[step], 0) for m, order in zip(messages, plan.orders)]

    def halve(states, step):
        cut = states[0][0].shape[0] // 2
        packed = [close_message(sums[:cut], counts[:cut]) for sums, counts in states]
        moved = [open_message(m, cut) for m in swap(packed, step)]
        return packed, [(s[cut:] + a, c[cut:] + b) for (s, c), (a, b) in zip(states, moved)]

    size = plan.chunk // 2
    got = swap(table(0, 2), 0)
    sent = table(1, 1)
    near = send(sent[0], 0, 1)
    far = [open_message(k + g, size) for k, g in zip(table(2, 2, after=sent), got)]
    gate = ()
    for step in range(1, plan.planes):
        packed, far = halve(far, step)
        gate = gate or packed
    sums = jnp.stack([s.reshape(2, plan.color, width) for s, _ in far], axis=1).reshape(2, plan.owned, width)
    counts = jnp.stack([c.reshape(2, plan.color) for _, c in far], axis=1).reshape(2, plan.owned)
    finals = [send(close_message(sums[i], counts[i]), 0, 2 + i) for i in range(2)]
    (kept,) = table(3, 1, after=gate)
    near = kept + near
    sums, counts = open_message(near, plan.chunk)
    sums = sums.reshape(2, 2, size // 2, width)
    counts = counts.reshape(2, 2, size // 2)
    states = [(sums[:, c].reshape(size, width), counts[:, c].reshape(size)) for c in range(2)]
    for step in range(plan.planes):
        _, states = halve(states, step)
    finals.append(close_message(jnp.concatenate([s for s, _ in states]), jnp.concatenate([c for _, c in states])))
    total = functools.reduce(jnp.add, finals)
    number = total[plan.owned :].reshape(-1)[: plan.owned]
    return total[: plan.owned] / jnp.maximum(number, 1.0)[:, None], number


def solution(mesh):
    plan = Plan(mesh)

    def body(*args):
        return shards(plan, *args)

    return jax.shard_map(
        body,
        mesh=mesh,
        in_specs=(
            P("section", "rows", None),
            P("section", "rows"),
            P("section", "rows"),
            P("section", None, "rows"),
            P("section", None, None),
            P("section", None),
        ),
        out_specs=(P(("section", "rows"), None), P(("section", "rows"))),
        check_vma=False,
    )
```

```python
import functools
import jax
import jax.numpy as jnp
from jax import lax
from jax.experimental import pallas as pl
from jax.experimental.pallas import tpu as pltpu
from jax.sharding import PartitionSpec as P


KEYS = 8192
STEP = 512
LEVEL = 1024
SECTIONS = 4
LANES = 128
BF16 = jnp.bfloat16
F32 = jnp.float32
VMEM = pl.BlockSpec(memory_space=pltpu.VMEM)
HBM = pl.BlockSpec(memory_space=pltpu.HBM)


def split(value):
    high = value.astype(BF16)
    return high, (value - high.astype(F32)).astype(BF16)


def iota(shape, axis):
    return lax.broadcasted_iota(jnp.int32, shape, axis)


class Plan:
    def __init__(self, mesh):
        self.sections = mesh.shape["section"]
        self.rows = mesh.shape["rows"]
        self.planes = self.rows.bit_length() - 2
        self.owned = KEYS // (self.sections * self.rows)
        self.color = self.owned // 2
        self.half = KEYS // 2
        self.chunk = self.half // 4
        bits = list(range(self.planes))
        turn = self.planes // 2
        self.orders = (bits, bits[turn:] + bits[:turn])

    def perm(self, row_xor, section_xor):
        return [
            (s * self.rows + r, (s ^ section_xor) * self.rows + (r ^ row_xor))
            for s in range(self.sections)
            for r in range(self.rows)
        ]


def slot_codes(plan, keys, z, p):
    log_color = plan.color.bit_length() - 1
    low = keys & (plan.color - 1)
    rest = keys >> log_color
    color = rest & 1
    core = (rest >> 1) & 1
    place = ((rest >> 2) & ((1 << plan.planes) - 1)) ^ p
    zrel = (rest >> (2 + plan.planes)) ^ z
    inner = []
    for order in plan.orders:
        index = 0
        for bit in order:
            index = index * 2 + (1 - ((place >> bit) & 1))
        inner.append(index)
    index = jnp.where(color == 0, inner[0], inner[1])
    count = 1 << (plan.planes - 1)
    kept = index >> (plan.planes - 1)
    index = index & (count - 1)
    far = ((color * count + index) * 2 + (zrel & 1)) * plan.color + 2 * plan.chunk * kept
    near = ((kept * 2 + color) * count + index) * plan.color + jnp.where(zrel == 1, plan.chunk, 3 * plan.chunk)
    return jnp.where(zrel >= 2, far, near) + low + core * plan.half


def fetch(pairs, sems):
    copies = [pltpu.make_async_copy(src, dst, sems.at[i]) for i, (src, dst) in enumerate(pairs)]
    for copy in copies:
        copy.start()
    return copies


def pack_kernel(plan, batches, predicates_hbm, weight_hbm, bias_hbm, *refs):
    buffers = refs[: plan.sections]
    predicates_ref, weight_ref, bias_ref, sems = refs[plan.sections :]
    copies = fetch(
        ((weight_hbm, weight_ref), (predicates_hbm, predicates_ref), (bias_hbm, bias_ref)),
        sems,
    )
    z = lax.axis_index("section")
    for copy in copies:
        copy.wait()
    width = weight_ref.shape[1]
    words_in_batch = predicates_ref.shape[2]
    for k, buffer in enumerate(buffers):
        buffer[:width, :] = weight_ref[0]
        buffer[width:, :] = jnp.zeros((buffer.shape[0] - width, width), F32)
        words = predicates_ref[0, pl.ds((z ^ k) * batches, batches), :]
        words = jnp.concatenate([words[m : m + 1] for m in range(batches)], axis=1)
        for b in range(4):
            at = width + b
            buffer[at : at + 1, : batches * words_in_batch] = ((words >> (8 * b)) & 255).astype(F32)
        buffer[width + 4 : width + 5, :] = bias_ref[...]


def advance_kernel(
    plan,
    x_hbm,
    keys_hbm,
    valid_hbm,
    b0,
    b1,
    b2,
    b3,
    out_ref,
    own_packed,
    own_lines,
    weight,
    bias,
    x_ref,
    keys_ref,
    valid_ref,
    bytes_,
    sparse,
    out_packed,
    out_lines,
    sems,
):
    batches, block, width = x_hbm.shape
    keys_copy, valid_copy, *x_copies = fetch(
        ((keys_hbm, keys_ref), (valid_hbm, valid_ref), *((x_hbm.at[m], x_ref.at[m]) for m in range(batches))),
        sems,
    )
    z = lax.axis_index("section")
    row = lax.axis_index("rows")
    core = row & 1
    place = row >> 1
    for k, buffer in enumerate((b0, b1, b2, b3)):
        level = z ^ k
        high, low = split(buffer[:width, :])
        weight[level, :width, :width] = high
        weight[level, width:, :width] = high
        weight[level, :width, width:] = low
        weight[level, width:, width:] = jnp.zeros_like(low)
        bytes_[level] = buffer[width : width + 8, :]
        bias[level, :1, :] = buffer[width + 4 : width + 5, :]
    words = bytes_[...].reshape(SECTIONS * 8, LANES)
    turned = [pltpu.roll(words, (LANES - m * (block // 32)) % LANES, axis=1) for m in range(batches)]
    words = jnp.concatenate(turned, axis=0).astype(BF16)
    lane = iota((1, block), 1)
    spread = (iota((LANES, block), 0) == (iota((LANES, block), 1) >> 5)).astype(F32).astype(BF16)
    found = jnp.dot(words, spread, preferred_element_type=F32).astype(jnp.int32)
    which = (lane >> 3) & 3
    keys_copy.wait()
    valid_copy.wait()
    tile = sparse.shape[2]
    per_batch = block // tile
    for m in range(batches):
        flags = []
        for s in range(SECTIONS):
            at = (m * SECTIONS + s) * 8
            byte = found[at : at + 1]
            for b in range(1, 4):
                byte = jnp.where(which == b, found[at + b : at + b + 1], byte)
            flags.append((byte >> (lane & 7)) & 1)
        depth = flags[-1]
        for flag in flags[-2::-1]:
            depth = flag * (1 + depth)
        depth = jnp.where(lane < valid_ref[:, m : m + 1], depth, 0).astype(F32)
        code = slot_codes(plan, keys_ref[m : m + 1, :], z, place).astype(F32)
        for q in range(per_batch):
            at = m * per_batch + q
            sparse[0, at : at + 1, :] = depth[:, q * tile : (q + 1) * tile]
            sparse[1, at : at + 1, :] = code[:, q * tile : (q + 1) * tile]

    depths = sparse[0]
    here = jnp.where(sparse[1] >= plan.half, 1.0, 0.0) == core.astype(F32)
    before = (iota((tile, tile), 0) < iota((tile, tile), 1)).astype(F32).astype(BF16)
    lists = []
    for same in (here, jnp.logical_not(here)):
        live = jnp.where(jnp.logical_and(depths > 0.0, same), 1.0, 0.0)
        places = jnp.dot(live.astype(BF16), before, preferred_element_type=F32)
        lists.append((live, jnp.where(live > 0.0, places, -1.0)))
    row8 = iota((8, tile), 0)
    lane8 = iota((8, LANES), 1)
    empty = jnp.where(iota((8, LANES), 0) == 0, -1.0, 0.0)
    packed, lines_refs = (own_packed, out_packed), (own_lines, out_lines)
    for lines_ref in lines_refs:
        for i in range(lines_ref.shape[0]):
            lines_ref[i] = empty
    offsets = [0, 0]
    for m in range(batches):
        x_copies[m].wait()
        for q in range(per_batch):
            at = m * per_batch + q
            spots = iota((tile, tile), 0).astype(F32)
            moves = [jnp.where(places[at : at + 1] == spots, 1.0, 0.0).astype(BF16) for _, places in lists]
            move = jnp.concatenate(moves, axis=0)
            both = jnp.concatenate(split(x_ref[m, q * tile : (q + 1) * tile, :]), axis=1)
            moved = jnp.dot(move, both, preferred_element_type=F32)
            moved = moved[:, :width] + moved[:, width:]
            code = sparse[1, at : at + 1, :] + 1.0
            high = jnp.floor(code * (1.0 / LANES))
            info = jnp.where(row8 == 0, high, jnp.where(row8 == 1, code - high * LANES, 0.0))
            info = jnp.where(row8 == 2, sparse[0, at : at + 1, :], info).astype(BF16)
            infos = lax.dot_general(info, move, (((1,), (1,)), ((), ())), preferred_element_type=F32)
            for l, (live, _) in enumerate(lists):
                offset = offsets[l]
                packed[l][pl.ds(offset, tile), :] = moved[l * tile : (l + 1) * tile]
                info = infos[:, l * tile : (l + 1) * tile]
                code = info[:1] * LANES + info[1:2] - 1.0
                info = jnp.where(row8 == 0, code, jnp.where(row8 == 1, info[2:3], 0.0))
                shift = offset & (LANES - 1)
                info = pltpu.roll(jnp.concatenate([info, empty], axis=1), shift, axis=1)
                line = offset // LANES
                lines_ref = lines_refs[l]
                lines_ref[line] = jnp.where(lane8 < shift, lines_ref[line], info[:, :LANES])
                for j in range(1, tile // LANES + 1):
                    lines_ref[line + j] = info[:, j * LANES : (j + 1) * LANES]
                number = jnp.sum(live[at : at + 1]).astype(jnp.int32)
                offsets[l] = pl.multiple_of(offset + ((number + 7) // 8) * 8, 8)
    for l in range(2):
        packed[l][pl.ds(offsets[l], LEVEL), :] = jnp.zeros((LEVEL, width), F32)
    used = jnp.full((8, width), offsets[0].astype(F32))
    own_lines[own_lines.shape[0] - 1] = used
    used = offsets[1]
    out_ref[out_ref.shape[0] - 8 :, :] = jnp.full((8, width), used.astype(F32))
    rows = batches * block
    lines = rows // LANES
    counts = out_ref.at[rows + lines : rows + lines + plan.half // LANES]
    run_levels(plan, rows, 1 - core, used, out_packed, out_lines, weight, bias, out_ref, counts)


def run_levels(plan, rows, core, used, packed, lines_ref, weight, bias, target, counts):
    width = target.shape[1]
    counts[...] = jnp.zeros(counts.shape, F32)

    def body(step, _):
        at = pl.multiple_of(step * LEVEL, LEVEL)
        columns, codes, depths = [], [], []
        for j in range(LEVEL // LANES):
            line = lines_ref[step * (LEVEL // LANES) + j]
            columns.append(jnp.broadcast_to(jnp.transpose(line)[:, 1:2], (LANES, width)))
            codes.append(line[:1])
            depths.append(line[1:2])
        depth = jnp.concatenate(columns, axis=0)
        code = jnp.concatenate(codes, axis=1).astype(jnp.int32) - core * plan.half
        outer = (iota((counts.shape[0], LEVEL), 0) == (code >> 7)).astype(F32).astype(BF16)
        inner = iota((LANES, LEVEL), 0) == (code & (LANES - 1))
        inner = jnp.where(inner, jnp.concatenate(depths, axis=1), 0.0).astype(BF16)
        counts[...] += lax.dot_general(outer, inner, (((1,), (1,)), ((), ())), preferred_element_type=F32)
        hidden = packed[pl.ds(at, LEVEL), :]
        total = jnp.zeros((LEVEL, width), F32)
        for s in range(SECTIONS):
            both = jnp.concatenate(split(hidden), axis=1)
            product = jnp.dot(both, weight[s], preferred_element_type=F32)
            hidden = hidden + jnp.tanh(product[:, :width] + product[:, width:] + bias[s, :1, :])
            total = total + jnp.where(depth > s, hidden, 0.0)
        target[pl.ds(at, LEVEL), :] = total
        return 0

    lax.fori_loop(0, (used + (LEVEL - 1)) // LEVEL, body, 0)
    for i in range(rows // LANES):
        target[rows + i : rows + i + 1, :] = lines_ref[i, :1, :]


def own_levels_kernel(plan, rows, packed, lines_ref, weight, bias, own_ref, counts):
    core = lax.axis_index("rows") & 1
    used = lines_ref[lines_ref.shape[0] - 1]
    own_ref[own_ref.shape[0] - 8 :, :] = used
    used = jnp.max(used).astype(jnp.int32)
    run_levels(plan, rows, core, used, packed, lines_ref, weight, bias, own_ref, counts)


def add_products(plan, rows, source, first, slots, sums):
    core = lax.axis_index("rows") & 1
    base = (core * plan.half + first).astype(F32)
    used = jnp.max(source[source.shape[0] - 8 :, :]).astype(jnp.int32)
    tile = min(256, slots)

    def body(step, _):
        at = pl.multiple_of(step * STEP, STEP)
        both = jnp.concatenate(split(source[pl.ds(at, STEP), :]), axis=1)
        codes = [source[pl.ds(rows + step * (STEP // LANES) + i, 1), :] - base for i in range(STEP // LANES)]
        for t in range(slots // tile):
            spots = (iota((tile, LANES), 0) + t * tile).astype(F32)
            marks = [jnp.where(code == spots, 1.0, 0.0).astype(BF16) for code in codes]
            mark = jnp.concatenate(marks, axis=1)
            sums[t * tile : (t + 1) * tile, :] += jnp.dot(mark, both, preferred_element_type=F32)
        return 0

    lax.fori_loop(0, (used + (STEP - 1)) // STEP, body, 0)


def own_kernel(plan, rows, own_ref, out_ref, sums):
    width = out_ref.shape[1]
    sums[...] = jnp.zeros_like(sums)
    add_products(plan, rows, own_ref, 0, sums.shape[0], sums)
    out_ref[...] = sums[:, :width] + sums[:, width:]


def table_kernel(plan, rows, start, early, other_ref, mine_ref, count_ref, *refs):
    *outs, sums = refs
    width = mine_ref.shape[1]
    size = plan.chunk // len(outs)
    lines = size // LANES
    at = rows + rows // LANES
    sums[...] = jnp.zeros_like(sums)
    if not early:
        add_products(plan, rows, mine_ref, start, plan.chunk, sums)
    add_products(plan, rows, other_ref, start, plan.chunk, sums)
    for i, out in enumerate(outs):
        low = i * size
        slot = start + low
        total = sums[low : low + size, :width] + sums[low : low + size, width:]
        out[:size, :] = total + mine_ref[slot : slot + size, :] if early else total
        line = slot // LANES
        out[size:, :] = count_ref[line : line + lines, :] + other_ref[at + line : at + line + lines, :]


def call(kernel, out_shape, operands, scratch=(), hbm=(), limit=24):
    return pl.pallas_call(
        kernel,
        out_shape=out_shape,
        in_specs=[HBM if i in hbm else VMEM for i in range(len(operands))],
        out_specs=jax.tree.map(lambda _: VMEM, out_shape),
        scratch_shapes=list(scratch),
        compiler_params=pltpu.CompilerParams(vmem_limit_bytes=limit << 20),
    )(*(pltpu.with_memory_space_constraint(o, pltpu.HBM) if i in hbm else o for i, o in enumerate(operands)))


def shape(*dims):
    return jax.ShapeDtypeStruct(dims, F32)


def lines_of(counts):
    return jnp.pad(counts, (0, -counts.shape[0] % LANES)).reshape(-1, LANES)


def shards(plan, rows_data, row_keys, valid_counts, predicates, section_weight, section_bias):
    batches, block, width = rows_data.shape
    axes = ("section", "rows")
    packed = call(
        functools.partial(pack_kernel, plan, batches),
        (shape(width + 8, width),) * plan.sections,
        (predicates, section_weight, section_bias),
        scratch=[
            pltpu.VMEM(predicates.shape, jnp.int32),
            pltpu.VMEM(section_weight.shape, F32),
            pltpu.VMEM(section_bias.shape, F32),
            pltpu.SemaphoreType.DMA((3,)),
        ],
        hbm=(0, 1, 2),
        limit=4,
    )
    buffers = [packed[0]]
    for k in range(1, plan.sections):
        buffers.append(lax.ppermute(packed[k], axes, plan.perm(0, k)))
    rows = batches * block
    lines = rows // LANES
    tables = plan.half // LANES
    tile = min(256, block)
    listed = (shape(rows + LEVEL, width), shape(lines + LEVEL // LANES + 1, 8, LANES))
    given, *mine = call(
        functools.partial(advance_kernel, plan),
        (
            shape(rows + lines + tables + 8, width),
            *listed,
            jax.ShapeDtypeStruct((SECTIONS, 2 * width, 2 * width), BF16),
            shape(SECTIONS, 8, width),
        ),
        (rows_data, row_keys, valid_counts.reshape(1, batches), *buffers),
        scratch=[
            pltpu.VMEM((batches, block, width), F32),
            pltpu.VMEM((batches, block), jnp.int32),
            pltpu.VMEM((1, batches), jnp.int32),
            pltpu.VMEM((SECTIONS, 8, LANES), F32),
            pltpu.VMEM((2, rows // tile, tile), F32),
            *(pltpu.VMEM(one.shape, F32) for one in listed),
            pltpu.SemaphoreType.DMA((batches + 2,)),
        ],
        hbm=(0, 1, 2),
    )
    other = lax.ppermute(given, axes, plan.perm(1, 0))
    own, count = call(
        functools.partial(own_levels_kernel, plan, rows), (shape(rows + lines + 8, width), shape(tables, LANES)), mine
    )
    part = call(
        functools.partial(own_kernel, plan, rows),
        shape(2 * plan.chunk, width),
        (own,),
        scratch=[pltpu.VMEM((2 * plan.chunk, 2 * width), F32)],
    )

    def table(chunk, messages, after=()):
        size = plan.chunk // messages
        early = chunk < 2
        operand, _ = lax.optimization_barrier((count, tuple(after)))
        return call(
            functools.partial(table_kernel, plan, rows, chunk * plan.chunk, early),
            (shape(size + size // LANES, width),) * messages,
            (other, part if early else own, operand),
            scratch=[pltpu.VMEM((plan.chunk, 2 * width), F32)],
        )

    def open_message(message, size):
        return message[:size], message[size:].reshape(-1)[:size]

    def close_message(sums, counts):
        return jnp.concatenate([sums, lines_of(counts)], axis=0)

    def send(message, row_xor, section_xor):
        return lax.ppermute(message, axes, plan.perm(row_xor, section_xor))

    def swap(messages, step):
        return [send(m, 2 << order[step], 0) for m, order in zip(messages, plan.orders)]

    def halve(states, step):
        cut = states[0][0].shape[0] // 2
        packed = [close_message(sums[:cut], counts[:cut]) for sums, counts in states]
        moved = [open_message(m, cut) for m in swap(packed, step)]
        return packed, [(s[cut:] + a, c[cut:] + b) for (s, c), (a, b) in zip(states, moved)]

    size = plan.chunk // 2
    got = swap(table(0, 2), 0)
    sent = table(1, 1)
    near = send(sent[0], 0, 1)
    far = [open_message(k + g, size) for k, g in zip(table(2, 2, after=sent), got)]
    gate = ()
    for step in range(1, plan.planes):
        packed, far = halve(far, step)
        gate = gate or packed
    sums = jnp.stack([s.reshape(2, plan.color, width) for s, _ in far], axis=1).reshape(2, plan.owned, width)
    counts = jnp.stack([c.reshape(2, plan.color) for _, c in far], axis=1).reshape(2, plan.owned)
    finals = [send(close_message(sums[i], counts[i]), 0, 2 + i) for i in range(2)]
    (kept,) = table(3, 1, after=gate)
    near = kept + near
    sums, counts = open_message(near, plan.chunk)
    sums = sums.reshape(2, 2, size // 2, width)
    counts = counts.reshape(2, 2, size // 2)
    states = [(sums[:, c].reshape(size, width), counts[:, c].reshape(size)) for c in range(2)]
    for step in range(plan.planes):
        _, states = halve(states, step)
    finals.append(close_message(jnp.concatenate([s for s, _ in states]), jnp.concatenate([c for _, c in states])))
    across = min(LANES, plan.owned)
    means, number = call(
        functools.partial(finish_kernel, plan),
        (shape(plan.owned, width), shape(plan.owned // across, across)),
        finals,
        limit=8,
    )
    return means, number.reshape(-1)


def finish_kernel(plan, *refs):
    *parts, means_ref, number_ref = refs
    total = functools.reduce(jnp.add, [part[: plan.owned, :] for part in parts])
    number = functools.reduce(jnp.add, [part[plan.owned :, :] for part in parts])
    number_ref[...] = number[:, : number_ref.shape[1]]
    columns = []
    for i in range(number.shape[0]):
        column = jnp.transpose(jnp.broadcast_to(jnp.maximum(number[i : i + 1], 1.0), (8, LANES)))
        columns.append(jnp.broadcast_to(column[:, :1], (LANES, total.shape[1])))
    means_ref[...] = total / jnp.concatenate(columns, axis=0)[: plan.owned]


def solution(mesh):
    plan = Plan(mesh)

    def body(*args):
        return shards(plan, *args)

    return jax.shard_map(
        body,
        mesh=mesh,
        in_specs=(
            P("section", "rows", None),
            P("section", "rows"),
            P("section", "rows"),
            P("section", None, "rows"),
            P("section", None, None),
            P("section", None),
        ),
        out_specs=(P(("section", "rows"), None), P(("section", "rows"))),
        check_vma=False,
    )
```

```python
import functools
import jax
import jax.numpy as jnp
from jax import lax
from jax.experimental import pallas as pl
from jax.experimental.pallas import tpu as pltpu
from jax.sharding import PartitionSpec as P


KEYS = 8192
STEP = 512
LEVEL = 1024
SECTIONS = 4
LANES = 128
BF16 = jnp.bfloat16
F32 = jnp.float32
VMEM = pl.BlockSpec(memory_space=pltpu.VMEM)
HBM = pl.BlockSpec(memory_space=pltpu.HBM)


def split(value):
    high = value.astype(BF16)
    return high, (value - high.astype(F32)).astype(BF16)


def iota(shape, axis):
    return lax.broadcasted_iota(jnp.int32, shape, axis)


class Plan:
    def __init__(self, mesh):
        self.sections = mesh.shape["section"]
        self.rows = mesh.shape["rows"]
        self.planes = self.rows.bit_length() - 2
        self.owned = KEYS // (self.sections * self.rows)
        self.color = self.owned // 2
        self.half = KEYS // 2
        self.chunk = self.half // 4
        bits = list(range(self.planes))
        turn = self.planes // 2
        self.orders = (bits, bits[turn:] + bits[:turn])

    def perm(self, row_xor, section_xor):
        return [
            (s * self.rows + r, (s ^ section_xor) * self.rows + (r ^ row_xor))
            for s in range(self.sections)
            for r in range(self.rows)
        ]


def slot_codes(plan, keys, z, p):
    log_color = plan.color.bit_length() - 1
    low = keys & (plan.color - 1)
    rest = keys >> log_color
    color = rest & 1
    core = (rest >> 1) & 1
    place = ((rest >> 2) & ((1 << plan.planes) - 1)) ^ p
    zrel = (rest >> (2 + plan.planes)) ^ z
    inner = []
    for order in plan.orders:
        index = 0
        for bit in order:
            index = index * 2 + (1 - ((place >> bit) & 1))
        inner.append(index)
    index = jnp.where(color == 0, inner[0], inner[1])
    count = 1 << (plan.planes - 1)
    kept = index >> (plan.planes - 1)
    index = index & (count - 1)
    far = ((color * count + index) * 2 + (zrel & 1)) * plan.color + 2 * plan.chunk * kept
    near = ((kept * 2 + color) * count + index) * plan.color + jnp.where(zrel == 1, plan.chunk, 3 * plan.chunk)
    return jnp.where(zrel >= 2, far, near) + low + core * plan.half


def fetch(pairs, sems):
    copies = [pltpu.make_async_copy(src, dst, sems.at[i]) for i, (src, dst) in enumerate(pairs)]
    for copy in copies:
        copy.start()
    return copies


def pack_kernel(plan, batches, predicates_hbm, weight_hbm, bias_hbm, *refs):
    buffers = refs[: plan.sections]
    predicates_ref, weight_ref, bias_ref, sems = refs[plan.sections :]
    copies = fetch(
        ((weight_hbm, weight_ref), (predicates_hbm, predicates_ref), (bias_hbm, bias_ref)),
        sems,
    )
    z = lax.axis_index("section")
    for copy in copies:
        copy.wait()
    width = weight_ref.shape[1]
    words_in_batch = predicates_ref.shape[2]
    for k, buffer in enumerate(buffers):
        buffer[:width, :] = weight_ref[0]
        buffer[width:, :] = jnp.zeros((buffer.shape[0] - width, width), F32)
        words = predicates_ref[0, pl.ds((z ^ k) * batches, batches), :]
        words = jnp.concatenate([words[m : m + 1] for m in range(batches)], axis=1)
        for b in range(4):
            at = width + b
            buffer[at : at + 1, : batches * words_in_batch] = ((words >> (8 * b)) & 255).astype(F32)
        buffer[width + 4 : width + 5, :] = bias_ref[...]


def prepare_kernel(plan, x_hbm, keys_hbm, both_ref, codes_ref, x_ref, keys_ref, sems):
    batches, block, width = x_hbm.shape
    keys_copy, *x_copies = fetch(
        ((keys_hbm, keys_ref), *((x_hbm.at[m], x_ref.at[m]) for m in range(batches))),
        sems,
    )
    z = lax.axis_index("section")
    place = lax.axis_index("rows") >> 1
    tile = codes_ref.shape[1]
    keys_copy.wait()
    for m in range(batches):
        code = slot_codes(plan, keys_ref[m : m + 1, :], z, place).astype(F32)
        for q in range(block // tile):
            at = m * (block // tile) + q
            codes_ref[at : at + 1, :] = code[:, q * tile : (q + 1) * tile]
    for m in range(batches):
        x_copies[m].wait()
        high, low = split(x_ref[m])
        both_ref[m * block : (m + 1) * block, :width] = high
        both_ref[m * block : (m + 1) * block, width:] = low


def advance_kernel(
    plan,
    batches,
    both_ref,
    codes_ref,
    valid_hbm,
    b0,
    b1,
    b2,
    b3,
    out_ref,
    own_packed,
    own_lines,
    weight,
    bias,
    valid_ref,
    bytes_,
    sparse,
    out_packed,
    out_lines,
    sems,
):
    block, width = both_ref.shape[0] // batches, both_ref.shape[1] // 2
    (valid_copy,) = fetch(((valid_hbm, valid_ref),), sems)
    z = lax.axis_index("section")
    row = lax.axis_index("rows")
    core = row & 1
    for k, buffer in enumerate((b0, b1, b2, b3)):
        level = z ^ k
        high, low = split(buffer[:width, :])
        weight[level, :width, :width] = high
        weight[level, width:, :width] = high
        weight[level, :width, width:] = low
        weight[level, width:, width:] = jnp.zeros_like(low)
        bytes_[level] = buffer[width : width + 8, :]
        bias[level, :1, :] = buffer[width + 4 : width + 5, :]
    words = bytes_[...].reshape(SECTIONS * 8, LANES)
    turned = [pltpu.roll(words, (LANES - m * (block // 32)) % LANES, axis=1) for m in range(batches)]
    words = jnp.concatenate(turned, axis=0).astype(BF16)
    lane = iota((1, block), 1)
    spread = (iota((LANES, block), 0) == (iota((LANES, block), 1) >> 5)).astype(F32).astype(BF16)
    found = jnp.dot(words, spread, preferred_element_type=F32).astype(jnp.int32)
    which = (lane >> 3) & 3
    valid_copy.wait()
    tile = sparse.shape[1]
    per_batch = block // tile
    for m in range(batches):
        flags = []
        for s in range(SECTIONS):
            at = (m * SECTIONS + s) * 8
            byte = found[at : at + 1]
            for b in range(1, 4):
                byte = jnp.where(which == b, found[at + b : at + b + 1], byte)
            flags.append((byte >> (lane & 7)) & 1)
        depth = flags[-1]
        for flag in flags[-2::-1]:
            depth = flag * (1 + depth)
        depth = jnp.where(lane < valid_ref[:, m : m + 1], depth, 0).astype(F32)
        for q in range(per_batch):
            at = m * per_batch + q
            sparse[at : at + 1, :] = depth[:, q * tile : (q + 1) * tile]

    depths = sparse[...]
    here = jnp.where(codes_ref[...] >= plan.half, 1.0, 0.0) == core.astype(F32)
    before = (iota((tile, tile), 0) < iota((tile, tile), 1)).astype(F32).astype(BF16)
    lists = []
    for same in (here, jnp.logical_not(here)):
        live = jnp.where(jnp.logical_and(depths > 0.0, same), 1.0, 0.0)
        places = jnp.dot(live.astype(BF16), before, preferred_element_type=F32)
        lists.append((live, jnp.where(live > 0.0, places, -1.0)))
    row8 = iota((8, tile), 0)
    lane8 = iota((8, LANES), 1)
    empty = jnp.where(iota((8, LANES), 0) == 0, -1.0, 0.0)
    packed, lines_refs = (own_packed, out_packed), (own_lines, out_lines)
    for lines_ref in lines_refs:
        for i in range(lines_ref.shape[0]):
            lines_ref[i] = empty
    offsets = [0, 0]
    for m in range(batches):
        for q in range(per_batch):
            at = m * per_batch + q
            spots = iota((tile, tile), 0).astype(F32)
            moves = [jnp.where(places[at : at + 1] == spots, 1.0, 0.0).astype(BF16) for _, places in lists]
            move = jnp.concatenate(moves, axis=0)
            both = both_ref[at * tile : (at + 1) * tile, :]
            moved = jnp.dot(move, both, preferred_element_type=F32)
            moved = moved[:, :width] + moved[:, width:]
            code = codes_ref[at : at + 1, :] + 1.0
            high = jnp.floor(code * (1.0 / LANES))
            info = jnp.where(row8 == 0, high, jnp.where(row8 == 1, code - high * LANES, 0.0))
            info = jnp.where(row8 == 2, sparse[at : at + 1, :], info).astype(BF16)
            infos = lax.dot_general(info, move, (((1,), (1,)), ((), ())), preferred_element_type=F32)
            for l, (live, _) in enumerate(lists):
                offset = offsets[l]
                packed[l][pl.ds(offset, tile), :] = moved[l * tile : (l + 1) * tile]
                info = infos[:, l * tile : (l + 1) * tile]
                code = info[:1] * LANES + info[1:2] - 1.0
                info = jnp.where(row8 == 0, code, jnp.where(row8 == 1, info[2:3], 0.0))
                shift = offset & (LANES - 1)
                info = pltpu.roll(jnp.concatenate([info, empty], axis=1), shift, axis=1)
                line = offset // LANES
                lines_ref = lines_refs[l]
                lines_ref[line] = jnp.where(lane8 < shift, lines_ref[line], info[:, :LANES])
                for j in range(1, tile // LANES + 1):
                    lines_ref[line + j] = info[:, j * LANES : (j + 1) * LANES]
                number = jnp.sum(live[at : at + 1]).astype(jnp.int32)
                offsets[l] = pl.multiple_of(offset + ((number + 7) // 8) * 8, 8)
    for l in range(2):
        packed[l][pl.ds(offsets[l], LEVEL), :] = jnp.zeros((LEVEL, width), F32)
    used = jnp.full((8, width), offsets[0].astype(F32))
    own_lines[own_lines.shape[0] - 1] = used
    used = offsets[1]
    out_ref[out_ref.shape[0] - 8 :, :] = jnp.full((8, width), used.astype(F32))
    rows = batches * block
    lines = rows // LANES
    counts = out_ref.at[rows + lines : rows + lines + plan.half // LANES]
    run_levels(plan, rows, 1 - core, used, out_packed, out_lines, weight, bias, out_ref, counts)


def run_levels(plan, rows, core, used, packed, lines_ref, weight, bias, target, counts):
    width = target.shape[1]
    counts[...] = jnp.zeros(counts.shape, F32)

    def body(step, _):
        at = pl.multiple_of(step * LEVEL, LEVEL)
        columns, codes, depths = [], [], []
        for j in range(LEVEL // LANES):
            line = lines_ref[step * (LEVEL // LANES) + j]
            columns.append(jnp.broadcast_to(jnp.transpose(line)[:, 1:2], (LANES, width)))
            codes.append(line[:1])
            depths.append(line[1:2])
        depth = jnp.concatenate(columns, axis=0)
        code = jnp.concatenate(codes, axis=1).astype(jnp.int32) - core * plan.half
        outer = (iota((counts.shape[0], LEVEL), 0) == (code >> 7)).astype(F32).astype(BF16)
        inner = iota((LANES, LEVEL), 0) == (code & (LANES - 1))
        inner = jnp.where(inner, jnp.concatenate(depths, axis=1), 0.0).astype(BF16)
        counts[...] += lax.dot_general(outer, inner, (((1,), (1,)), ((), ())), preferred_element_type=F32)
        hidden = packed[pl.ds(at, LEVEL), :]
        total = jnp.zeros((LEVEL, width), F32)
        for s in range(SECTIONS):
            both = jnp.concatenate(split(hidden), axis=1)
            product = jnp.dot(both, weight[s], preferred_element_type=F32)
            hidden = hidden + jnp.tanh(product[:, :width] + product[:, width:] + bias[s, :1, :])
            total = total + jnp.where(depth > s, hidden, 0.0)
        target[pl.ds(at, LEVEL), :] = total
        return 0

    lax.fori_loop(0, (used + (LEVEL - 1)) // LEVEL, body, 0)
    for i in range(rows // LANES):
        target[rows + i : rows + i + 1, :] = lines_ref[i, :1, :]


def own_levels_kernel(plan, rows, packed, lines_ref, weight, bias, own_ref, counts):
    core = lax.axis_index("rows") & 1
    used = lines_ref[lines_ref.shape[0] - 1]
    own_ref[own_ref.shape[0] - 8 :, :] = used
    used = jnp.max(used).astype(jnp.int32)
    run_levels(plan, rows, core, used, packed, lines_ref, weight, bias, own_ref, counts)


def add_products(plan, rows, source, first, slots, sums):
    core = lax.axis_index("rows") & 1
    base = (core * plan.half + first).astype(F32)
    used = jnp.max(source[source.shape[0] - 8 :, :]).astype(jnp.int32)
    tile = min(256, slots)

    def body(step, _):
        at = pl.multiple_of(step * STEP, STEP)
        both = jnp.concatenate(split(source[pl.ds(at, STEP), :]), axis=1)
        codes = [source[pl.ds(rows + step * (STEP // LANES) + i, 1), :] - base for i in range(STEP // LANES)]
        for t in range(slots // tile):
            spots = (iota((tile, LANES), 0) + t * tile).astype(F32)
            marks = [jnp.where(code == spots, 1.0, 0.0).astype(BF16) for code in codes]
            mark = jnp.concatenate(marks, axis=1)
            sums[t * tile : (t + 1) * tile, :] += jnp.dot(mark, both, preferred_element_type=F32)
        return 0

    lax.fori_loop(0, (used + (STEP - 1)) // STEP, body, 0)


def own_kernel(plan, rows, own_ref, out_ref, sums):
    width = out_ref.shape[1]
    sums[...] = jnp.zeros_like(sums)
    add_products(plan, rows, own_ref, 0, sums.shape[0], sums)
    out_ref[...] = sums[:, :width] + sums[:, width:]


def table_kernel(plan, rows, start, early, other_ref, mine_ref, count_ref, *refs):
    *outs, sums = refs
    width = mine_ref.shape[1]
    size = plan.chunk // len(outs)
    lines = size // LANES
    at = rows + rows // LANES
    sums[...] = jnp.zeros_like(sums)
    if not early:
        add_products(plan, rows, mine_ref, start, plan.chunk, sums)
    add_products(plan, rows, other_ref, start, plan.chunk, sums)
    for i, out in enumerate(outs):
        low = i * size
        slot = start + low
        total = sums[low : low + size, :width] + sums[low : low + size, width:]
        out[:size, :] = total + mine_ref[slot : slot + size, :] if early else total
        line = slot // LANES
        out[size:, :] = count_ref[line : line + lines, :] + other_ref[at + line : at + line + lines, :]


def call(kernel, out_shape, operands, scratch=(), hbm=(), limit=24):
    return pl.pallas_call(
        kernel,
        out_shape=out_shape,
        in_specs=[HBM if i in hbm else VMEM for i in range(len(operands))],
        out_specs=jax.tree.map(lambda _: VMEM, out_shape),
        scratch_shapes=list(scratch),
        compiler_params=pltpu.CompilerParams(vmem_limit_bytes=limit << 20),
    )(*(pltpu.with_memory_space_constraint(o, pltpu.HBM) if i in hbm else o for i, o in enumerate(operands)))


def shape(*dims):
    return jax.ShapeDtypeStruct(dims, F32)


def lines_of(counts):
    return jnp.pad(counts, (0, -counts.shape[0] % LANES)).reshape(-1, LANES)


def shards(plan, rows_data, row_keys, valid_counts, predicates, section_weight, section_bias):
    batches, block, width = rows_data.shape
    axes = ("section", "rows")
    packed = call(
        functools.partial(pack_kernel, plan, batches),
        (shape(width + 8, width),) * plan.sections,
        (predicates, section_weight, section_bias),
        scratch=[
            pltpu.VMEM(predicates.shape, jnp.int32),
            pltpu.VMEM(section_weight.shape, F32),
            pltpu.VMEM(section_bias.shape, F32),
            pltpu.SemaphoreType.DMA((3,)),
        ],
        hbm=(0, 1, 2),
        limit=4,
    )
    buffers = [packed[0]]
    for k in range(1, plan.sections):
        buffers.append(lax.ppermute(packed[k], axes, plan.perm(0, k)))
    rows = batches * block
    lines = rows // LANES
    tables = plan.half // LANES
    tile = min(256, block)
    listed = (shape(rows + LEVEL, width), shape(lines + LEVEL // LANES + 1, 8, LANES))
    both, codes = call(
        functools.partial(prepare_kernel, plan),
        (jax.ShapeDtypeStruct((rows, 2 * width), BF16), shape(rows // tile, tile)),
        (rows_data, row_keys),
        scratch=[
            pltpu.VMEM((batches, block, width), F32),
            pltpu.VMEM((batches, block), jnp.int32),
            pltpu.SemaphoreType.DMA((batches + 1,)),
        ],
        hbm=(0, 1),
        limit=8,
    )
    given, *mine = call(
        functools.partial(advance_kernel, plan, batches),
        (
            shape(rows + lines + tables + 8, width),
            *listed,
            jax.ShapeDtypeStruct((SECTIONS, 2 * width, 2 * width), BF16),
            shape(SECTIONS, 8, width),
        ),
        (both, codes, valid_counts.reshape(1, batches), *buffers),
        scratch=[
            pltpu.VMEM((1, batches), jnp.int32),
            pltpu.VMEM((SECTIONS, 8, LANES), F32),
            pltpu.VMEM((rows // tile, tile), F32),
            *(pltpu.VMEM(one.shape, F32) for one in listed),
            pltpu.SemaphoreType.DMA((1,)),
        ],
        hbm=(2,),
    )
    other = lax.ppermute(given, axes, plan.perm(1, 0))
    own, count = call(
        functools.partial(own_levels_kernel, plan, rows), (shape(rows + lines + 8, width), shape(tables, LANES)), mine
    )
    part = call(
        functools.partial(own_kernel, plan, rows),
        shape(2 * plan.chunk, width),
        (own,),
        scratch=[pltpu.VMEM((2 * plan.chunk, 2 * width), F32)],
    )

    def table(chunk, messages, after=()):
        size = plan.chunk // messages
        early = chunk < 2
        operand, _ = lax.optimization_barrier((count, tuple(after)))
        return call(
            functools.partial(table_kernel, plan, rows, chunk * plan.chunk, early),
            (shape(size + size // LANES, width),) * messages,
            (other, part if early else own, operand),
            scratch=[pltpu.VMEM((plan.chunk, 2 * width), F32)],
        )

    def open_message(message, size):
        return message[:size], message[size:].reshape(-1)[:size]

    def close_message(sums, counts):
        return jnp.concatenate([sums, lines_of(counts)], axis=0)

    def send(message, row_xor, section_xor):
        return lax.ppermute(message, axes, plan.perm(row_xor, section_xor))

    def swap(messages, step):
        return [send(m, 2 << order[step], 0) for m, order in zip(messages, plan.orders)]

    def halve(states, step):
        cut = states[0][0].shape[0] // 2
        packed = [close_message(sums[:cut], counts[:cut]) for sums, counts in states]
        moved = [open_message(m, cut) for m in swap(packed, step)]
        return packed, [(s[cut:] + a, c[cut:] + b) for (s, c), (a, b) in zip(states, moved)]

    size = plan.chunk // 2
    got = swap(table(0, 2), 0)
    sent = table(1, 1)
    near = send(sent[0], 0, 1)
    far = [open_message(k + g, size) for k, g in zip(table(2, 2, after=sent), got)]
    gate = ()
    for step in range(1, plan.planes):
        packed, far = halve(far, step)
        gate = gate or packed
    sums = jnp.stack([s.reshape(2, plan.color, width) for s, _ in far], axis=1).reshape(2, plan.owned, width)
    counts = jnp.stack([c.reshape(2, plan.color) for _, c in far], axis=1).reshape(2, plan.owned)
    finals = [send(close_message(sums[i], counts[i]), 0, 2 + i) for i in range(2)]
    (kept,) = table(3, 1, after=gate)
    near = kept + near
    sums, counts = open_message(near, plan.chunk)
    sums = sums.reshape(2, 2, size // 2, width)
    counts = counts.reshape(2, 2, size // 2)
    states = [(sums[:, c].reshape(size, width), counts[:, c].reshape(size)) for c in range(2)]
    for step in range(plan.planes):
        _, states = halve(states, step)
    finals.append(close_message(jnp.concatenate([s for s, _ in states]), jnp.concatenate([c for _, c in states])))
    across = min(LANES, plan.owned)
    means, number = call(
        functools.partial(finish_kernel, plan),
        (shape(plan.owned, width), shape(plan.owned // across, across)),
        finals,
        limit=8,
    )
    return means, number.reshape(-1)


def finish_kernel(plan, *refs):
    *parts, means_ref, number_ref = refs
    total = functools.reduce(jnp.add, [part[: plan.owned, :] for part in parts])
    number = functools.reduce(jnp.add, [part[plan.owned :, :] for part in parts])
    number_ref[...] = number[:, : number_ref.shape[1]]
    columns = []
    for i in range(number.shape[0]):
        column = jnp.transpose(jnp.broadcast_to(jnp.maximum(number[i : i + 1], 1.0), (8, LANES)))
        columns.append(jnp.broadcast_to(column[:, :1], (LANES, total.shape[1])))
    means_ref[...] = total / jnp.concatenate(columns, axis=0)[: plan.owned]


def solution(mesh):
    plan = Plan(mesh)

    def body(*args):
        return shards(plan, *args)

    return jax.shard_map(
        body,
        mesh=mesh,
        in_specs=(
            P("section", "rows", None),
            P("section", "rows"),
            P("section", "rows"),
            P("section", None, "rows"),
            P("section", None, None),
            P("section", None),
        ),
        out_specs=(P(("section", "rows"), None), P(("section", "rows"))),
        check_vma=False,
    )
```

```python
import functools
import jax
import jax.numpy as jnp
from jax import lax
from jax.experimental import pallas as pl
from jax.experimental.pallas import tpu as pltpu
from jax.sharding import PartitionSpec as P


KEYS = 8192
STEP = 512
LEVEL = 1024
SECTIONS = 4
LANES = 128
BF16 = jnp.bfloat16
F32 = jnp.float32
VMEM = pl.BlockSpec(memory_space=pltpu.VMEM)
HBM = pl.BlockSpec(memory_space=pltpu.HBM)


def split(value):
    high = value.astype(BF16)
    return high, (value - high.astype(F32)).astype(BF16)


def iota(shape, axis):
    return lax.broadcasted_iota(jnp.int32, shape, axis)


class Plan:
    def __init__(self, mesh):
        self.sections = mesh.shape["section"]
        self.rows = mesh.shape["rows"]
        self.planes = self.rows.bit_length() - 2
        self.owned = KEYS // (self.sections * self.rows)
        self.color = self.owned // 2
        self.half = KEYS // 2
        self.chunk = self.half // 4
        bits = list(range(self.planes))
        turn = self.planes // 2
        self.orders = (bits, bits[turn:] + bits[:turn])

    def perm(self, row_xor, section_xor):
        return [
            (s * self.rows + r, (s ^ section_xor) * self.rows + (r ^ row_xor))
            for s in range(self.sections)
            for r in range(self.rows)
        ]


def slot_codes(plan, keys, z, p):
    log_color = plan.color.bit_length() - 1
    low = keys & (plan.color - 1)
    rest = keys >> log_color
    color = rest & 1
    core = (rest >> 1) & 1
    place = ((rest >> 2) & ((1 << plan.planes) - 1)) ^ p
    zrel = (rest >> (2 + plan.planes)) ^ z
    inner = []
    for order in plan.orders:
        index = 0
        for bit in order:
            index = index * 2 + (1 - ((place >> bit) & 1))
        inner.append(index)
    index = jnp.where(color == 0, inner[0], inner[1])
    count = 1 << (plan.planes - 1)
    kept = index >> (plan.planes - 1)
    index = index & (count - 1)
    far = ((color * count + index) * 2 + (zrel & 1)) * plan.color + 2 * plan.chunk * kept
    near = ((kept * 2 + color) * count + index) * plan.color + jnp.where(zrel == 1, plan.chunk, 3 * plan.chunk)
    return jnp.where(zrel >= 2, far, near) + low + core * plan.half


def fetch(pairs, sems):
    copies = [pltpu.make_async_copy(src, dst, sems.at[i]) for i, (src, dst) in enumerate(pairs)]
    for copy in copies:
        copy.start()
    return copies


def pack_kernel(plan, batches, predicates_hbm, weight_hbm, bias_hbm, *refs):
    buffers = refs[: plan.sections]
    predicates_ref, weight_ref, bias_ref, sems = refs[plan.sections :]
    copies = fetch(
        ((weight_hbm, weight_ref), (predicates_hbm, predicates_ref), (bias_hbm, bias_ref)),
        sems,
    )
    z = lax.axis_index("section")
    for copy in copies:
        copy.wait()
    width = weight_ref.shape[1]
    words_in_batch = predicates_ref.shape[2]
    for k, buffer in enumerate(buffers):
        buffer[:width, :] = weight_ref[0]
        buffer[width:, :] = jnp.zeros((buffer.shape[0] - width, width), F32)
        words = predicates_ref[0, pl.ds((z ^ k) * batches, batches), :]
        words = jnp.concatenate([words[m : m + 1] for m in range(batches)], axis=1)
        for b in range(4):
            at = width + b
            buffer[at : at + 1, : batches * words_in_batch] = ((words >> (8 * b)) & 255).astype(F32)
        buffer[width + 4 : width + 5, :] = bias_ref[...]


def prepare_kernel(plan, x_hbm, keys_hbm, both_ref, codes_ref, x_ref, keys_ref, sems):
    batches, block, width = x_hbm.shape
    keys_copy, *x_copies = fetch(
        ((keys_hbm, keys_ref), *((x_hbm.at[m], x_ref.at[m]) for m in range(batches))),
        sems,
    )
    z = lax.axis_index("section")
    place = lax.axis_index("rows") >> 1
    tile = codes_ref.shape[1]
    keys_copy.wait()
    for m in range(batches):
        code = slot_codes(plan, keys_ref[m : m + 1, :], z, place).astype(F32)
        for q in range(block // tile):
            at = m * (block // tile) + q
            codes_ref[at : at + 1, :] = code[:, q * tile : (q + 1) * tile]
    for m in range(batches):
        x_copies[m].wait()
        high, low = split(x_ref[m])
        both_ref[m * block : (m + 1) * block, :width] = high
        both_ref[m * block : (m + 1) * block, width:] = low


def advance_kernel(
    plan,
    batches,
    both_ref,
    codes_ref,
    valid_hbm,
    b0,
    b1,
    b2,
    b3,
    out_ref,
    own_packed,
    own_lines,
    weight,
    bias,
    valid_ref,
    bytes_,
    sparse,
    out_packed,
    out_lines,
    sems,
):
    block, width = both_ref.shape[0] // batches, both_ref.shape[1] // 2
    (valid_copy,) = fetch(((valid_hbm, valid_ref),), sems)
    z = lax.axis_index("section")
    row = lax.axis_index("rows")
    core = row & 1
    for k, buffer in enumerate((b0, b1, b2, b3)):
        level = z ^ k
        high, low = split(buffer[:width, :])
        weight[level, :width, :width] = high
        weight[level, width:, :width] = high
        weight[level, :width, width:] = low
        weight[level, width:, width:] = jnp.zeros_like(low)
        bytes_[level] = buffer[width : width + 8, :]
        bias[level, :1, :] = buffer[width + 4 : width + 5, :]
    words = bytes_[...].reshape(SECTIONS * 8, LANES)
    turned = [pltpu.roll(words, (LANES - m * (block // 32)) % LANES, axis=1) for m in range(batches)]
    words = jnp.concatenate(turned, axis=0).astype(BF16)
    lane = iota((1, block), 1)
    spread = (iota((LANES, block), 0) == (iota((LANES, block), 1) >> 5)).astype(F32).astype(BF16)
    found = jnp.dot(words, spread, preferred_element_type=F32).astype(jnp.int32)
    which = (lane >> 3) & 3
    valid_copy.wait()
    tile = sparse.shape[1]
    per_batch = block // tile
    for m in range(batches):
        flags = []
        for s in range(SECTIONS):
            at = (m * SECTIONS + s) * 8
            byte = found[at : at + 1]
            for b in range(1, 4):
                byte = jnp.where(which == b, found[at + b : at + b + 1], byte)
            flags.append((byte >> (lane & 7)) & 1)
        depth = flags[-1]
        for flag in flags[-2::-1]:
            depth = flag * (1 + depth)
        depth = jnp.where(lane < valid_ref[:, m : m + 1], depth, 0).astype(F32)
        for q in range(per_batch):
            at = m * per_batch + q
            sparse[at : at + 1, :] = depth[:, q * tile : (q + 1) * tile]

    depths = sparse[...]
    here = jnp.where(codes_ref[...] >= plan.half, 1.0, 0.0) == core.astype(F32)
    before = (iota((tile, tile), 0) < iota((tile, tile), 1)).astype(F32).astype(BF16)
    lists = []
    for same in (here, jnp.logical_not(here)):
        live = jnp.where(jnp.logical_and(depths > 0.0, same), 1.0, 0.0)
        places = jnp.dot(live.astype(BF16), before, preferred_element_type=F32)
        lists.append((live, jnp.where(live > 0.0, places, -1.0)))
    row8 = iota((8, tile), 0)
    lane8 = iota((8, LANES), 1)
    empty = jnp.where(iota((8, LANES), 0) == 0, -1.0, 0.0)
    packed, lines_refs = (own_packed, out_packed), (own_lines, out_lines)
    for lines_ref in lines_refs:
        for i in range(lines_ref.shape[0]):
            lines_ref[i] = empty
    offsets = [0, 0]
    for m in range(batches):
        for q in range(per_batch):
            at = m * per_batch + q
            spots = iota((tile, tile), 0).astype(F32).astype(BF16)
            moves = [
                jnp.where(places[at : at + 1].astype(BF16) == spots, BF16(1.0), BF16(0.0)) for _, places in lists
            ]
            move = jnp.concatenate(moves, axis=0)
            both = both_ref[at * tile : (at + 1) * tile, :]
            moved = jnp.dot(move, both, preferred_element_type=F32)
            moved = moved[:, :width] + moved[:, width:]
            code = codes_ref[at : at + 1, :] + 1.0
            high = jnp.floor(code * (1.0 / LANES))
            info = jnp.where(row8 == 0, high, jnp.where(row8 == 1, code - high * LANES, 0.0))
            info = jnp.where(row8 == 2, sparse[at : at + 1, :], info).astype(BF16)
            infos = lax.dot_general(info, move, (((1,), (1,)), ((), ())), preferred_element_type=F32)
            for l, (live, _) in enumerate(lists):
                offset = offsets[l]
                packed[l][pl.ds(offset, tile), :] = moved[l * tile : (l + 1) * tile]
                info = infos[:, l * tile : (l + 1) * tile]
                code = info[:1] * LANES + info[1:2] - 1.0
                info = jnp.where(row8 == 0, code, jnp.where(row8 == 1, info[2:3], 0.0))
                shift = offset & (LANES - 1)
                info = pltpu.roll(jnp.concatenate([info, empty], axis=1), shift, axis=1)
                line = offset // LANES
                lines_ref = lines_refs[l]
                lines_ref[line] = jnp.where(lane8 < shift, lines_ref[line], info[:, :LANES])
                for j in range(1, tile // LANES + 1):
                    lines_ref[line + j] = info[:, j * LANES : (j + 1) * LANES]
                number = jnp.sum(live[at : at + 1]).astype(jnp.int32)
                offsets[l] = pl.multiple_of(offset + ((number + 7) // 8) * 8, 8)
    for l in range(2):
        packed[l][pl.ds(offsets[l], LEVEL), :] = jnp.zeros((LEVEL, width), F32)
    used = jnp.full((8, width), offsets[0].astype(F32))
    own_lines[own_lines.shape[0] - 1] = used
    used = offsets[1]
    out_ref[out_ref.shape[0] - 8 :, :] = jnp.full((8, width), used.astype(F32))
    rows = batches * block
    lines = rows // LANES
    counts = out_ref.at[rows + lines : rows + lines + plan.half // LANES]
    run_levels(plan, rows, 1 - core, used, out_packed, out_lines, weight, bias, out_ref, counts)


def run_levels(plan, rows, core, used, packed, lines_ref, weight, bias, target, counts):
    width = target.shape[1]
    counts[...] = jnp.zeros(counts.shape, F32)

    def body(step, _):
        at = pl.multiple_of(step * LEVEL, LEVEL)
        columns, codes, depths = [], [], []
        for j in range(LEVEL // LANES):
            line = lines_ref[step * (LEVEL // LANES) + j]
            columns.append(jnp.broadcast_to(jnp.transpose(line)[:, 1:2], (LANES, width)))
            codes.append(line[:1])
            depths.append(line[1:2])
        depth = jnp.concatenate(columns, axis=0)
        code = jnp.concatenate(codes, axis=1).astype(jnp.int32) - core * plan.half
        outer = (iota((counts.shape[0], LEVEL), 0) == (code >> 7)).astype(F32).astype(BF16)
        inner = iota((LANES, LEVEL), 0) == (code & (LANES - 1))
        inner = jnp.where(inner, jnp.concatenate(depths, axis=1), 0.0).astype(BF16)
        counts[...] += lax.dot_general(outer, inner, (((1,), (1,)), ((), ())), preferred_element_type=F32)
        hidden = packed[pl.ds(at, LEVEL), :]
        total = jnp.zeros((LEVEL, width), F32)
        for s in range(SECTIONS):
            both = jnp.concatenate(split(hidden), axis=1)
            product = jnp.dot(both, weight[s], preferred_element_type=F32)
            hidden = hidden + jnp.tanh(product[:, :width] + product[:, width:] + bias[s, :1, :])
            total = total + jnp.where(depth > s, hidden, 0.0)
        target[pl.ds(at, LEVEL), :] = total
        return 0

    lax.fori_loop(0, (used + (LEVEL - 1)) // LEVEL, body, 0)
    for i in range(rows // LANES):
        target[rows + i : rows + i + 1, :] = lines_ref[i, :1, :]


def own_levels_kernel(plan, rows, packed, lines_ref, weight, bias, own_ref, counts):
    core = lax.axis_index("rows") & 1
    used = lines_ref[lines_ref.shape[0] - 1]
    own_ref[own_ref.shape[0] - 8 :, :] = used
    used = jnp.max(used).astype(jnp.int32)
    run_levels(plan, rows, core, used, packed, lines_ref, weight, bias, own_ref, counts)


def add_products(plan, rows, source, first, slots, sums):
    core = lax.axis_index("rows") & 1
    base = (core * plan.half + first).astype(F32)
    used = jnp.max(source[source.shape[0] - 8 :, :]).astype(jnp.int32)
    tile = min(256, slots)

    def body(step, _):
        at = pl.multiple_of(step * STEP, STEP)
        both = jnp.concatenate(split(source[pl.ds(at, STEP), :]), axis=1)
        codes = [source[pl.ds(rows + step * (STEP // LANES) + i, 1), :] - base for i in range(STEP // LANES)]
        for t in range(slots // tile):
            spots = (iota((tile, LANES), 0) + t * tile).astype(F32)
            marks = [jnp.where(code == spots, 1.0, 0.0).astype(BF16) for code in codes]
            mark = jnp.concatenate(marks, axis=1)
            sums[t * tile : (t + 1) * tile, :] += jnp.dot(mark, both, preferred_element_type=F32)
        return 0

    lax.fori_loop(0, (used + (STEP - 1)) // STEP, body, 0)


def own_kernel(plan, rows, own_ref, out_ref, sums):
    width = out_ref.shape[1]
    sums[...] = jnp.zeros_like(sums)
    add_products(plan, rows, own_ref, 0, sums.shape[0], sums)
    out_ref[...] = sums[:, :width] + sums[:, width:]


def table_kernel(plan, rows, start, early, other_ref, mine_ref, count_ref, *refs):
    *outs, sums = refs
    width = mine_ref.shape[1]
    size = plan.chunk // len(outs)
    lines = size // LANES
    at = rows + rows // LANES
    sums[...] = jnp.zeros_like(sums)
    if not early:
        add_products(plan, rows, mine_ref, start, plan.chunk, sums)
    add_products(plan, rows, other_ref, start, plan.chunk, sums)
    for i, out in enumerate(outs):
        low = i * size
        slot = start + low
        total = sums[low : low + size, :width] + sums[low : low + size, width:]
        out[:size, :] = total + mine_ref[slot : slot + size, :] if early else total
        line = slot // LANES
        out[size:, :] = count_ref[line : line + lines, :] + other_ref[at + line : at + line + lines, :]


def call(kernel, out_shape, operands, scratch=(), hbm=(), limit=24):
    return pl.pallas_call(
        kernel,
        out_shape=out_shape,
        in_specs=[HBM if i in hbm else VMEM for i in range(len(operands))],
        out_specs=jax.tree.map(lambda _: VMEM, out_shape),
        scratch_shapes=list(scratch),
        compiler_params=pltpu.CompilerParams(vmem_limit_bytes=limit << 20),
    )(*(pltpu.with_memory_space_constraint(o, pltpu.HBM) if i in hbm else o for i, o in enumerate(operands)))


def shape(*dims):
    return jax.ShapeDtypeStruct(dims, F32)


def lines_of(counts):
    return jnp.pad(counts, (0, -counts.shape[0] % LANES)).reshape(-1, LANES)


def shards(plan, rows_data, row_keys, valid_counts, predicates, section_weight, section_bias):
    batches, block, width = rows_data.shape
    axes = ("section", "rows")
    packed = call(
        functools.partial(pack_kernel, plan, batches),
        (shape(width + 8, width),) * plan.sections,
        (predicates, section_weight, section_bias),
        scratch=[
            pltpu.VMEM(predicates.shape, jnp.int32),
            pltpu.VMEM(section_weight.shape, F32),
            pltpu.VMEM(section_bias.shape, F32),
            pltpu.SemaphoreType.DMA((3,)),
        ],
        hbm=(0, 1, 2),
        limit=4,
    )
    buffers = [packed[0]]
    for k in range(1, plan.sections):
        buffers.append(lax.ppermute(packed[k], axes, plan.perm(0, k)))
    rows = batches * block
    lines = rows // LANES
    tables = plan.half // LANES
    tile = min(256, block)
    listed = (shape(rows + LEVEL, width), shape(lines + LEVEL // LANES + 1, 8, LANES))
    both, codes = call(
        functools.partial(prepare_kernel, plan),
        (jax.ShapeDtypeStruct((rows, 2 * width), BF16), shape(rows // tile, tile)),
        (rows_data, row_keys),
        scratch=[
            pltpu.VMEM((batches, block, width), F32),
            pltpu.VMEM((batches, block), jnp.int32),
            pltpu.SemaphoreType.DMA((batches + 1,)),
        ],
        hbm=(0, 1),
        limit=8,
    )
    given, *mine = call(
        functools.partial(advance_kernel, plan, batches),
        (
            shape(rows + lines + tables + 8, width),
            *listed,
            jax.ShapeDtypeStruct((SECTIONS, 2 * width, 2 * width), BF16),
            shape(SECTIONS, 8, width),
        ),
        (both, codes, valid_counts.reshape(1, batches), *buffers),
        scratch=[
            pltpu.VMEM((1, batches), jnp.int32),
            pltpu.VMEM((SECTIONS, 8, LANES), F32),
            pltpu.VMEM((rows // tile, tile), F32),
            *(pltpu.VMEM(one.shape, F32) for one in listed),
            pltpu.SemaphoreType.DMA((1,)),
        ],
        hbm=(2,),
    )
    other = lax.ppermute(given, axes, plan.perm(1, 0))
    own, count = call(
        functools.partial(own_levels_kernel, plan, rows), (shape(rows + lines + 8, width), shape(tables, LANES)), mine
    )
    part = call(
        functools.partial(own_kernel, plan, rows),
        shape(2 * plan.chunk, width),
        (own,),
        scratch=[pltpu.VMEM((2 * plan.chunk, 2 * width), F32)],
    )

    def table(chunk, messages, after=()):
        size = plan.chunk // messages
        early = chunk < 2
        operand, _ = lax.optimization_barrier((count, tuple(after)))
        return call(
            functools.partial(table_kernel, plan, rows, chunk * plan.chunk, early),
            (shape(size + size // LANES, width),) * messages,
            (other, part if early else own, operand),
            scratch=[pltpu.VMEM((plan.chunk, 2 * width), F32)],
        )

    def open_message(message, size):
        return message[:size], message[size:].reshape(-1)[:size]

    def close_message(sums, counts):
        return jnp.concatenate([sums, lines_of(counts)], axis=0)

    def send(message, row_xor, section_xor):
        return lax.ppermute(message, axes, plan.perm(row_xor, section_xor))

    def swap(messages, step):
        return [send(m, 2 << order[step], 0) for m, order in zip(messages, plan.orders)]

    def halve(states, step):
        cut = states[0][0].shape[0] // 2
        packed = [close_message(sums[:cut], counts[:cut]) for sums, counts in states]
        moved = [open_message(m, cut) for m in swap(packed, step)]
        return packed, [(s[cut:] + a, c[cut:] + b) for (s, c), (a, b) in zip(states, moved)]

    size = plan.chunk // 2
    got = swap(table(0, 2), 0)
    sent = table(1, 1)
    near = send(sent[0], 0, 1)
    far = [open_message(k + g, size) for k, g in zip(table(2, 2, after=sent), got)]
    gate = ()
    for step in range(1, plan.planes):
        packed, far = halve(far, step)
        gate = gate or packed
    sums = jnp.stack([s.reshape(2, plan.color, width) for s, _ in far], axis=1).reshape(2, plan.owned, width)
    counts = jnp.stack([c.reshape(2, plan.color) for _, c in far], axis=1).reshape(2, plan.owned)
    finals = [send(close_message(sums[i], counts[i]), 0, 2 + i) for i in range(2)]
    (kept,) = table(3, 1, after=gate)
    near = kept + near
    sums, counts = open_message(near, plan.chunk)
    sums = sums.reshape(2, 2, size // 2, width)
    counts = counts.reshape(2, 2, size // 2)
    states = [(sums[:, c].reshape(size, width), counts[:, c].reshape(size)) for c in range(2)]
    for step in range(plan.planes):
        _, states = halve(states, step)
    finals.append(close_message(jnp.concatenate([s for s, _ in states]), jnp.concatenate([c for _, c in states])))
    across = min(LANES, plan.owned)
    means, number = call(
        functools.partial(finish_kernel, plan),
        (shape(plan.owned, width), shape(plan.owned // across, across)),
        finals,
        limit=8,
    )
    return means, number.reshape(-1)


def finish_kernel(plan, *refs):
    *parts, means_ref, number_ref = refs
    total = functools.reduce(jnp.add, [part[: plan.owned, :] for part in parts])
    number = functools.reduce(jnp.add, [part[plan.owned :, :] for part in parts])
    number_ref[...] = number[:, : number_ref.shape[1]]
    columns = []
    for i in range(number.shape[0]):
        column = jnp.transpose(jnp.broadcast_to(jnp.maximum(number[i : i + 1], 1.0), (8, LANES)))
        columns.append(jnp.broadcast_to(column[:, :1], (LANES, total.shape[1])))
    means_ref[...] = total / jnp.concatenate(columns, axis=0)[: plan.owned]


def solution(mesh):
    plan = Plan(mesh)

    def body(*args):
        return shards(plan, *args)

    return jax.shard_map(
        body,
        mesh=mesh,
        in_specs=(
            P("section", "rows", None),
            P("section", "rows"),
            P("section", "rows"),
            P("section", None, "rows"),
            P("section", None, None),
            P("section", None),
        ),
        out_specs=(P(("section", "rows"), None), P(("section", "rows"))),
        check_vma=False,
    )
```
